32 devices in a mesh: ctx: 16 (over z, y, core), tp: 2 (over x).
Axes of the slice: x: 2, y: 2, z: 4, core: 2. Of those that a mesh axis runs over, the one named last changes fastest.
Arguments:
- q_proj: bfloat16 [4096, 4096], P('ctx', 'tp'), may hold values from -6 to 6
- k_proj: bfloat16 [4096, 1024], P('ctx', 'tp'), may hold values from -6 to 6
- v_proj: bfloat16 [4096, 1024], P('ctx', 'tp'), may hold values from -6 to 6
- out_grad: bfloat16 [4096, 4096], P('ctx', 'tp'), may hold values from -6 to 6
- o_weight: bfloat16 [4096, 4096], P('ctx', 'tp'), may hold values from -0.09375 to 0.09375
- doc_extra: int32 [8], replicated, may hold values from 1 to 768, 2048 in all
Outputs:
- q_grad: bfloat16 [4096, 4096], P('ctx', 'tp')
- k_grad: bfloat16 [4096, 1024], P('ctx', 'tp')
- v_grad: bfloat16 [4096, 1024], P('ctx', 'tp')
The draws below stay inside these ranges and needn't reach their ends.
Inputs may be any that keep to these rules, and one draw needn't show every extreme that they name: `doc_extra`: the extra lengths sum to 2048, so the documents fill the sequence; the longest document has exactly 1024 tokens.
All inputs are finite; a program needn't handle non-finite values.
Results may differ from the reference program's by a relative error of at most 0.011.
Values may be sent and summed in bfloat16 or wider, within the bound.
A program may use at most 128 MiB of HBM per device.

```python
import math
import jax
import jax.numpy as jnp
import numpy as np
from jax import lax

D = 4096
H = 32
KVH = 8
HD = 128
T_DEV = 256
DOC_MIN = 256
DOC_MAX = 1024
TOKENS = 4096
NDOC = 8
REACH = 4


def draw_q_proj(key, part):
    shape_full = (TOKENS, KVH, H // KVH, HD)
    full = jnp.clip(jax.random.normal(jax.random.fold_in(key, 1), shape_full), -6.0, 6.0)
    return full.reshape(TOKENS, H * HD).astype(jnp.float32).astype(jnp.bfloat16)


def draw_k_proj(key, part):
    shape_full = (TOKENS, KVH, HD)
    full = jnp.clip(jax.random.normal(jax.random.fold_in(key, 3), shape_full), -6.0, 6.0)
    return full.reshape(TOKENS, KVH * HD).astype(jnp.float32).astype(jnp.bfloat16)


def level_of(key, dims, shards, smallest, high):
    factor_of, own = 1.0, jax.random.fold_in(key, 6)
    for dim, parts in shards:
        steps = jnp.exp(jax.random.uniform(jax.random.fold_in(own, dim), (parts,), jnp.float32, smallest / len(shards), high / len(shards)))
        factor_of = factor_of * jnp.repeat(steps, dims[dim] // parts).reshape([-1 if axis == dim else 1 for axis in range(len(dims))])
    return factor_of


def split_up(number_of, total, reach, slope):
    weights = [(1 << 20) // math.isqrt(standing ** slope) + 1 for standing in range(2, number_of + 1)]
    rest, counts = total - reach - (number_of - 1), [1] * (number_of - 1)
    while rest > 0:
        movable = [i for i in range(number_of - 1) if counts[i] < reach]
        whole, left = sum([weights[i] for i in movable]), rest
        for i in movable:
            extra = min(reach - counts[i], max(1, left * weights[i] // whole), rest)
            counts[i] = counts[i] + extra
            rest = rest - extra
    return np.array([reach] + counts)


def uneven(rng, number_of, total, most, lean):
    if number_of == 2:
        one = jax.random.randint(rng, (), max(1, total - most), min(most, total - 1) + 1)
        return jnp.stack([one, total - one])
    tallies = jnp.asarray(split_up(number_of, total, most, lean), jnp.int32)
    pairs = (number_of - 1) // 2
    donor, taker = tallies[1:1 + 2 * pairs:2], tallies[2:2 + 2 * pairs:2]
    slack = jnp.minimum(donor - 1, most - taker)
    shifted = jax.random.randint(jax.random.fold_in(rng, 1), (pairs,), 0, 1 << 20) % (slack + 1)
    tallies = tallies.at[1:1 + 2 * pairs:2].set(donor - shifted).at[2:2 + 2 * pairs:2].set(taker + shifted)
    return tallies[jax.random.permutation(jax.random.fold_in(rng, 2), number_of)]


def noise(key, shape, deviation, most, pieces=(), held_as=jnp.bfloat16):
    array = jax.random.normal(key, shape, jnp.float32) * deviation
    if len(pieces) > 0:
        array = level_of(key, shape, pieces, -0.22, 0.18) * array
    return jnp.clip(array, min=-most, max=most).astype(held_as)


def setup_inputs(seed: int = 0) -> dict:
    key_of = jax.random.split(jax.random.key(seed), 7)
    return {
        "q_proj": draw_q_proj(jax.random.fold_in(key_of[6], 71), 0),
        "k_proj": draw_k_proj(jax.random.fold_in(key_of[6], 71), 0),
        "v_proj": noise(key_of[2], (TOKENS, KVH * HD), 1.0, 6.0, ((0, 16), (1, 2))),
        "out_grad": noise(key_of[3], (TOKENS, D), 1.0, 6.0, ((0, 16), (1, 2))),
        "o_weight": noise(key_of[4], (D, H * HD), (H * HD) ** -0.5, 0.09375, ((0, 16), (1, 2))),
        "doc_extra": uneven(key_of[5], NDOC, TOKENS - DOC_MIN * NDOC, DOC_MAX - DOC_MIN, 2).astype(jnp.int32),
    }


NEG_FILL = -1e+30

def reference(q_proj, k_proj, v_proj, out_grad, o_weight, doc_extra):
    scaling = 1.0 / math.sqrt(HD)
    q_group = H // KVH
    margin = REACH * T_DEV
    window = margin + T_DEV
    head_all = jnp.dot(out_grad, o_weight, preferred_element_type=jnp.float32).astype(jnp.bfloat16)
    doc_starts = DOC_MIN * jnp.arange(NDOC, dtype=jnp.int32) + jnp.cumsum(doc_extra, dtype=jnp.int32) - doc_extra
    position = jnp.arange(TOKENS, dtype=jnp.int32)
    doc_first = lax.optimization_barrier(jnp.max(jnp.where(doc_starts[None, :] <= position[:, None], doc_starts[None, :], 0), axis=1))
    zero_rows = jnp.zeros((margin, KVH * HD), jnp.bfloat16)
    key_pad = jnp.concatenate([zero_rows, k_proj], axis=0)
    val_pad = jnp.concatenate([zero_rows, v_proj], axis=0)
    own_rows = jnp.arange(window, dtype=jnp.int32) >= margin
    highest = lax.Precision.HIGHEST

    def one_block(running, block_id):
        k_acc, v_acc = running
        row_start = (block_id * T_DEV).astype(jnp.int32)
        queries = lax.dynamic_slice_in_dim(q_proj, row_start, T_DEV, 0).reshape(T_DEV, KVH, q_group, HD).astype(jnp.float32)
        head_grad = lax.dynamic_slice_in_dim(head_all, row_start, T_DEV, 0).reshape(T_DEV, KVH, q_group, HD).astype(jnp.float32)
        key_block = lax.dynamic_slice_in_dim(key_pad, row_start, window, 0).reshape(window, KVH, HD).astype(jnp.float32)
        val_block = lax.dynamic_slice_in_dim(val_pad, row_start, window, 0).reshape(window, KVH, HD).astype(jnp.float32)
        q_pos = row_start + jnp.arange(T_DEV, dtype=jnp.int32)
        key_pos = row_start - margin + jnp.arange(window, dtype=jnp.int32)
        q_first = lax.dynamic_slice_in_dim(doc_first, row_start, T_DEV, 0)
        allowed = (key_pos[None, :] >= q_first[:, None]) & (key_pos[None, :] <= q_pos[:, None])
        raw_scores = jnp.einsum('tgqd,kgd->gqtk', queries, key_block, precision=highest) * scaling
        masked = jnp.where(allowed, raw_scores, NEG_FILL)
        row_peak = lax.optimization_barrier(jnp.max(masked, axis=-1))
        log_total = row_peak + jnp.log(lax.optimization_barrier(jnp.sum(jnp.exp(masked - row_peak[..., None]), axis=-1)))
        soft = jnp.where(allowed, jnp.exp(raw_scores - log_total[..., None]), 0.0)
        soft_bf = soft.astype(jnp.bfloat16).astype(jnp.float32)
        attn_out = jnp.einsum('gqtk,kgd->gqtd', soft_bf, val_block, precision=highest)
        delta = lax.optimization_barrier(jnp.sum(head_grad.transpose(1, 2, 0, 3) * attn_out, axis=-1))
        dprob = jnp.einsum('tgqd,kgd->gqtk', head_grad, val_block, precision=highest)
        dscore = (soft * (dprob - delta[..., None])).astype(jnp.bfloat16).astype(jnp.float32)
        q_part = jnp.einsum('gqtk,kgd->tgqd', dscore, key_block, precision=highest) * scaling
        k_part = jnp.einsum('gqtk,tgqd->kgd', dscore, queries, precision=highest) * scaling
        v_part = jnp.einsum('gqtk,tgqd->kgd', soft_bf, head_grad, precision=highest)
        k_round = lax.optimization_barrier(k_part.astype(jnp.bfloat16)).astype(jnp.float32)
        v_round = lax.optimization_barrier(v_part.astype(jnp.bfloat16)).astype(jnp.float32)
        k_part = jnp.where(own_rows[:, None, None], k_part, k_round)
        v_part = jnp.where(own_rows[:, None, None], v_part, v_round)
        k_acc = lax.dynamic_update_slice_in_dim(k_acc, lax.dynamic_slice_in_dim(k_acc, row_start, window, 0) + k_part, row_start, 0)
        v_acc = lax.dynamic_update_slice_in_dim(v_acc, lax.dynamic_slice_in_dim(v_acc, row_start, window, 0) + v_part, row_start, 0)
        return ((k_acc, v_acc), q_part.astype(jnp.bfloat16).reshape(T_DEV, H * HD))
    start_acc = jnp.zeros((TOKENS + margin, KVH, HD), jnp.float32)
    finals, q_blocks = lax.scan(one_block, (start_acc, start_acc), jnp.arange(TOKENS // T_DEV, dtype=jnp.int32))
    k_acc, v_acc = finals
    q_grad = q_blocks.reshape(TOKENS, H * HD)
    k_grad = k_acc[margin:].reshape(TOKENS, KVH * HD).astype(jnp.bfloat16)
    v_grad = v_acc[margin:].reshape(TOKENS, KVH * HD).astype(jnp.bfloat16)
    return (q_grad, k_grad, v_grad)
```

```python
import functools
import math

import jax
import jax.numpy as jnp
from jax import lax
from jax.experimental import pallas as pl
from jax.experimental.pallas import tpu as pltpu
from jax.sharding import PartitionSpec as P

H = 32
KVH = 8
HD = 128
DOC_MIN = 256
DOC_MAX = 1024


NEG_FILL = -1e30


def shifted(value, axis, steps):
    count = lax.axis_size(axis)
    leading, last = (max(0, -steps), min(count, count - steps))
    return lax.ppermute(value, axis, [(source, source + steps) for source in range(leading, last)])


def keep_state(state):
    return state


def local(q_proj, k_proj, v_proj, out_grad, o_weight, doc_extra):
    tok_rows = q_proj.shape[0]
    kv_local = k_proj.shape[1] // HD
    q_group = H // KVH
    scaling = 1.0 / math.sqrt(HD)
    reach = DOC_MAX // tok_rows
    dev_index = lax.axis_index("ctx")
    gathered = lax.all_gather(out_grad, "tp", axis=1, tiled=True)
    head_sum = jnp.dot(
        gathered,
        lax.all_gather(o_weight, "ctx", axis=0, tiled=True),
        preferred_element_type=jnp.float32,
    )
    head_grad = head_sum.astype(jnp.bfloat16).reshape(tok_rows, kv_local, q_group, HD)
    queries = q_proj.reshape(tok_rows, kv_local, q_group, HD)
    order = jnp.arange(doc_extra.shape[0], dtype=jnp.int32)
    earlier = order[:, None] > order[None, :]
    doc_starts = jnp.sum(jnp.where(earlier, DOC_MIN + doc_extra[None, :], 0), axis=1)
    position = dev_index * tok_rows + jnp.arange(tok_rows, dtype=jnp.int32)
    doc_first = jnp.max(
        jnp.where(doc_starts[None, :] <= position[:, None], doc_starts[None, :], 0), axis=1
    )
    stacked = jnp.stack([k_proj, v_proj])
    sources = [stacked]
    moving = stacked
    for offset in range(1, reach + 1):
        moving = shifted(moving, "ctx", 1)
        sources.append(moving)

    def scores_for(source, offset):
        key_block = source[0].reshape(tok_rows, kv_local, HD)
        raw_scores = (
            jnp.einsum("tgqd,kgd->gqtk", queries, key_block, preferred_element_type=jnp.float32)
            * scaling
        )
        key_pos = (dev_index - offset) * tok_rows + jnp.arange(tok_rows, dtype=jnp.int32)
        allowed = (key_pos[None, :] >= doc_first[:, None]) & (key_pos[None, :] <= position[:, None])
        return (raw_scores, allowed)

    def is_live(offset):
        return (dev_index - offset >= 0) & (doc_first[0] <= (dev_index - offset + 1) * tok_rows - 1)

    raw_scores, allowed = scores_for(sources[0], 0)
    masked = jnp.where(allowed, raw_scores, NEG_FILL)
    row_peak = jnp.max(masked, axis=-1)
    row_total = jnp.sum(jnp.exp(masked - row_peak[..., None]), axis=-1)
    for offset in range(1, reach + 1):

        def merge_block(state):
            old_peak, old_total = state
            scores_new, allowed_new = scores_for(sources[offset], offset)
            masked_new = jnp.where(allowed_new, scores_new, NEG_FILL)
            new_peak = jnp.maximum(old_peak, jnp.max(masked_new, axis=-1))
            new_total = old_total * jnp.exp(old_peak - new_peak) + jnp.sum(
                jnp.exp(masked_new - new_peak[..., None]), axis=-1
            )
            return (new_peak, new_total)

        row_peak, row_total = lax.cond(
            is_live(offset), merge_block, keep_state, (row_peak, row_total)
        )
    log_total = row_peak + jnp.log(row_total)

    def soft_weights(source, offset):
        scores_here, allowed_here = scores_for(source, offset)
        return jnp.where(allowed_here, jnp.exp(scores_here - log_total[..., None]), 0.0)

    def add_output(running, source, offset):
        soft_bf = soft_weights(source, offset).astype(jnp.bfloat16)
        val_block = source[1].reshape(tok_rows, kv_local, HD)
        return running + jnp.einsum(
            "gqtk,kgd->gqtd", soft_bf, val_block, preferred_element_type=jnp.float32
        )

    attn_out = add_output(jnp.zeros((kv_local, q_group, tok_rows, HD), jnp.float32), sources[0], 0)
    for offset in range(1, reach + 1):

        def add_live(running):
            return add_output(running, sources[offset], offset)

        attn_out = lax.cond(is_live(offset), add_live, keep_state, attn_out)
    delta = jnp.sum(head_grad.transpose(1, 2, 0, 3).astype(jnp.float32) * attn_out, axis=-1)

    def grads_for(source, offset):
        key_block = source[0].reshape(tok_rows, kv_local, HD)
        val_block = source[1].reshape(tok_rows, kv_local, HD)
        soft = soft_weights(source, offset)
        soft_bf = soft.astype(jnp.bfloat16)
        dprob = jnp.einsum(
            "tgqd,kgd->gqtk", head_grad, val_block, preferred_element_type=jnp.float32
        )
        dscore = (soft * (dprob - delta[..., None])).astype(jnp.bfloat16)
        q_part = jnp.einsum("gqtk,kgd->tgqd", dscore, key_block, preferred_element_type=jnp.float32)
        k_part = (
            jnp.einsum("gqtk,tgqd->kgd", dscore, queries, preferred_element_type=jnp.float32)
            * scaling
        )
        v_part = jnp.einsum(
            "gqtk,tgqd->kgd", soft_bf, head_grad, preferred_element_type=jnp.float32
        )
        return (q_part, k_part, v_part)

    q_acc, k_acc, v_acc = grads_for(sources[0], 0)
    for offset in range(1, reach + 1):

        def live_grads(unused):
            return grads_for(sources[offset], offset)

        def no_grads(unused):
            return (jnp.zeros_like(q_acc), jnp.zeros_like(k_acc), jnp.zeros_like(v_acc))

        q_add, k_add, v_add = lax.cond(is_live(offset), live_grads, no_grads, 0)
        q_acc = q_acc + q_add
        sent = jnp.stack([k_add, v_add]).astype(jnp.bfloat16).reshape(2, tok_rows, kv_local * HD)
        returned = shifted(sent, "ctx", -offset)
        k_acc = k_acc + returned[0].astype(jnp.float32).reshape(tok_rows, kv_local, HD)
        v_acc = v_acc + returned[1].astype(jnp.float32).reshape(tok_rows, kv_local, HD)
    q_grad = (q_acc * scaling).astype(jnp.bfloat16).reshape(tok_rows, kv_local * q_group * HD)
    k_grad = k_acc.astype(jnp.bfloat16).reshape(tok_rows, kv_local * HD)
    v_grad = v_acc.astype(jnp.bfloat16).reshape(tok_rows, kv_local * HD)
    return (q_grad, k_grad, v_grad)


GROUP = 4
STORE_PARTS = 4
CHUNKS = ((0, 2), (2, 2))
PARTS = len(CHUNKS)
MESH = pl.DeviceIdType.MESH


def place():
    me, t = lax.axis_index("ctx"), lax.axis_index("tp")
    return me, t, me // GROUP, me % GROUP


def send(src, dst, send_sem, recv_sem, device):
    return pltpu.make_async_remote_copy(
        src_ref=src, dst_ref=dst, send_sem=send_sem, recv_sem=recv_sem,
        device_id=device, device_id_type=MESH,
    )


def arrived(ref, sem):
    pltpu.make_async_copy(ref, ref, sem).wait()


def greet(devices, groups, g, t):
    barrier = pltpu.get_barrier_semaphore()

    def signal(device):
        pl.semaphore_signal(barrier, inc=1, device_id=device, device_id_type=MESH)

    for device in devices:
        signal(device)

    @pl.when(g > 0)
    def _():
        for member in range(GROUP):
            signal(((g - 1) * GROUP + member, t))

    @pl.when(g < groups - 1)
    def _():
        for member in range(GROUP):
            signal(((g + 1) * GROUP + member, t))

    inner = jnp.where((g > 0) & (g < groups - 1), GROUP, 0)
    pl.semaphore_wait(barrier, len(devices) + GROUP + inner)


def step_kernel(
    groups, rows, q, k, v, og, w, extra, q_grad, k_grad, v_grad,
    ogb, wb, acc, head_grad, q_out, kv_out, stash, attn, sums, dq, back, returned, final, owned,
    local_sem, w_send, w_recv, up_send, down_send, og_send, og_recv, q_send, q_recv,
    kv_send, kv_recv, far_send, far_recv,
    dq_send, dq_recv, back_send, back_recv, fin_send, fin_recv, home_sem,
):
    me, t, g, l = place()
    base = g * GROUP
    wide, span = q.shape[1] // GROUP, GROUP * rows
    depth = w.shape[0]
    unit = ogb.shape[2]
    x_dev, y_l, c_l = (me, 1 - t), (l + 2) % GROUP, l + 1 - 2 * (l % 2)
    core = l % 2
    far_chip = 2 - 2 * (l // 2)
    peers = [l, c_l, far_chip, far_chip + 1]
    y_dev, c_dev = (base + y_l, t), (base + c_l, t)
    above, below = (me + GROUP, t), (me - GROUP, t)
    greet([(base + peers[j], t) for j in (1, 2, 3)] + [x_dev], groups, g, t)

    def cols(ref, index, size):
        return ref.at[:, pl.ds(pl.multiple_of(index * size, size), size)]

    def lanes_of(ch):
        return pl.ds(CHUNKS[ch][0] * HD, CHUNKS[ch][1] * HD)

    def slab_piece(group, member, ch):
        return wb[ch].at[group, pl.ds(pl.multiple_of(member * depth, depth), depth)]

    def w_cols(member, ch):
        first, count = CHUNKS[ch]
        return w.at[:, pl.ds(pl.multiple_of(member * wide + first * HD, HD), count * HD)]

    def w_sem(group, member, ch):
        return w_recv.at[(group * GROUP + member) * PARTS + ch]

    def token_rows(ref, member):
        return ref.at[pl.ds(pl.multiple_of(member * rows, rows), rows)]

    def og_unit(tt, member, u):
        return ogb.at[tt * 2 + u, pl.ds(pl.multiple_of(member * rows, rows), rows)]

    def og_own(u):
        return og.at[:, pl.ds(u * unit, unit)]

    def og_sem(tt, member, u):
        return og_recv.at[(tt * GROUP + member) * 2 + u]

    def kv_rows(which, member):
        return kv_out.at[which, pl.ds(pl.multiple_of(span + member * rows, rows), rows)]

    sends, locals_ = [], []

    def go(copy):
        copy.start()
        sends.append(copy)

    def stay(src, dst):
        copy = pltpu.make_async_copy(src, dst, local_sem.at[len(locals_)])
        copy.start()
        locals_.append(copy)

    def up_copy(src, group, member, step, j, ch):
        return send(src, slab_piece(group, member, ch), up_send.at[(step * GROUP + j) * PARTS + ch],
                    w_sem(group, member, ch), above)

    def down_copy(src, group, member, step, j, ch):
        return send(src, slab_piece(group, member, ch), down_send.at[(step * GROUP + j) * PARTS + ch],
                    w_sem(group, member, ch), below)

    def own_send(ch):
        @pl.when(g < groups - 1)
        def _():
            up_copy(w_cols(l, ch), g, l, 0, 0, ch).start()

        @pl.when(g > 0)
        def _():
            down_copy(w_cols(l, ch), g, l, 0, 0, ch).start()

    @pl.when(core == 0)
    def _():
        for ch in range(PARTS):
            own_send(ch)

    def w_to(j):
        for ch in range(PARTS):
            go(send(w_cols(peers[j], ch), slab_piece(g, l, ch), w_send.at[(j - 1) * PARTS + ch],
                    w_sem(g, l, ch), (base + peers[j], t)))

    w_to(2)
    w_to(1)
    for which, ref in ((0, k), (1, v)):
        for j in (1, 2, 3):
            go(send(cols(ref, peers[j], HD), kv_rows(which, l), kv_send.at[which * 3 + j - 1],
                    kv_recv.at[which * GROUP + l], (base + peers[j], t)))
        stay(cols(ref, l, HD), kv_rows(which, l))
    w_to(3)
    for u in (0, 1):
        go(send(og_own(u), og_unit(t, l, u), og_send.at[u], og_sem(t, l, u), x_dev))
    for ch in range(PARTS):
        stay(w_cols(l, ch), slab_piece(g, l, ch))
    for u in (0, 1):
        go(send(og_own(u), og_unit(t, l, u), og_send.at[4 + u], og_sem(t, l, u), c_dev))
        stay(og_own(u), og_unit(t, l, u))
    go(send(og_own(1), og_unit(t, l, 1), og_send.at[2], og_sem(t, l, 1), y_dev))
    for j in (1, 2, 3):
        go(send(cols(q, peers[j], wide), token_rows(q_out, l), q_send.at[j - 1],
                q_recv.at[l], (base + peers[j], t)))
    go(send(og_own(0), og_unit(t, l, 0), og_send.at[3], og_sem(t, l, 0), y_dev))
    stay(cols(q, l, wide), token_rows(q_out, l))

    @pl.when(g == 0)
    def _():
        kv_out[:, 0:span] = jnp.zeros((2, span, HD), kv_out.dtype)

    sums[...] = jnp.zeros_like(sums)

    def forward(step, ch):
        if step == 0:
            for j in range(1, GROUP):
                piece = slab_piece(g, peers[j], ch)
                arrived(piece, w_sem(g, peers[j], ch))

                @pl.when(g < groups - 1)
                def _():
                    up_copy(piece, g, peers[j], 0, j, ch).start()

                @pl.when(g > 0)
                def _():
                    down_copy(piece, g, peers[j], 0, j, ch).start()
        else:
            for j in range(GROUP):
                @pl.when((g >= step) & (g < groups - 1))
                def _():
                    piece = slab_piece(g - step, peers[j], ch)
                    arrived(piece, w_sem(g - step, peers[j], ch))
                    up_copy(piece, g - step, peers[j], step, j, ch).start()

                @pl.when((g + step < groups) & (g > 0))
                def _():
                    piece = slab_piece(g + step, peers[j], ch)
                    arrived(piece, w_sem(g + step, peers[j], ch))
                    down_copy(piece, g + step, peers[j], step, j, ch).start()

    def collect(step, ch):
        @pl.when((g >= step) & (g == groups - 1))
        def _():
            for j in range(GROUP):
                arrived(slab_piece(g - step, peers[j], ch), w_sem(g - step, peers[j], ch))

        @pl.when((g + step < groups) & (g == 0))
        def _():
            for j in range(GROUP):
                arrived(slab_piece(g + step, peers[j], ch), w_sem(g + step, peers[j], ch))

    last_slab = jnp.where(2 * g < groups, groups - 1, 0)
    early_slabs = [(last_slab + 1 + n) % groups for n in range(groups - 1)]

    def project(ch, terms, begin, finish):
        lanes = lanes_of(ch)

        @pl.loop(0, GROUP)
        def _(i):
            part = pl.ds(pl.multiple_of(i * rows, rows), rows)
            total = acc[part, lanes] if not begin else 0.0
            for slab in terms:
                total = total + jnp.dot(
                    ogb[slab, part], wb[ch][slab], preferred_element_type=jnp.float32)
            if finish:
                head_grad[part, lanes] = total.astype(head_grad.dtype)
            else:
                acc[part, lanes] = total

    def og_pass(tt, member, u, index, device):
        return send(og_unit(tt, member, u), og_unit(tt, member, u), og_send.at[index],
                    og_sem(tt, member, u), device)

    def og_onward(tt, member, u):
        if tt is not t:
            if member is l:
                onward = [og_pass(tt, member, u, 8 + u, c_dev)]
                return onward + ([og_pass(tt, member, 0, 6, y_dev)] if u == 0 else [])
            return [og_pass(tt, member, u, 12 + u, c_dev)]
        onward = [og_pass(tt, member, u, 10 + u, c_dev)]
        return onward + ([og_pass(tt, member, 1, 7, x_dev)] if u == 1 else [])

    other = 1 - t
    og_arrivals = [(tt, member, u) for tt, member in ((other, l), (t, y_l), (other, y_l))
                   for u in (0, 1)]

    def og_relay(tt, member, u):
        arrived(og_unit(tt, member, u), og_sem(tt, member, u))
        for copy in og_onward(tt, member, u):
            copy.start()

    def og_last():
        for member in (c_l, (c_l + 2) % GROUP):
            for tt in (t, 1 - t):
                for u in (0, 1):
                    arrived(og_unit(tt, member, u), og_sem(tt, member, u))

    def far_copy():
        return send(kv_out.at[:, pl.ds(span, span)], kv_out.at[:, pl.ds(0, span)],
                    far_send, far_recv, above)

    window = (GROUP + 1) * rows
    heads = wide // HD
    scaling = 1.0 / math.sqrt(HD)
    column = lax.broadcasted_iota(jnp.int32, (window, rows), 0)
    row = lax.broadcasted_iota(jnp.int32, (window, rows), 1)
    causal = column <= span + row
    lane = lax.broadcasted_iota(jnp.int32, (1, rows), 1)

    def first_of(i):
        position = g * span + i * rows + lane
        start, found = jnp.int32(0), jnp.zeros((1, rows), jnp.int32)
        for j in range(extra.shape[0]):
            found = jnp.where(position >= start, start, found)
            start = start + DOC_MIN + extra[j]
        return found

    def dot(a, b, dims):
        return lax.dot_general(a, b, ((dims[:1], dims[1:]), ((), ())),
                               preferred_element_type=jnp.float32)

    def softmax_block(i):
        part, keys = pl.ds(i * rows, rows), pl.ds(i * rows, window)
        kw = kv_out[0, keys]
        vw_t = kv_out[1, keys].T
        allowed = causal & (column >= first_of(i) - ((g - 1) * span + i * rows))
        for h in range(heads):
            score = jnp.where(allowed, dot(kw, q_out[part, pl.ds(h * HD, HD)], (1, 1)), NEG_FILL)
            expd = jnp.exp((score - jnp.max(score, axis=0, keepdims=True)) * scaling)
            prob = expd * (1.0 / jnp.sum(expd, axis=0, keepdims=True))
            prob_bf = prob.astype(stash.dtype)
            stash[i * heads + h] = prob_bf
            attn[i * heads + h] = dot(vw_t, prob_bf, (1, 0))

    def keys_ready():
        for which in (0, 1):
            for j in (1, 2, 3):
                arrived(kv_rows(which, peers[j]), kv_recv.at[which * GROUP + peers[j]])
        for copy in locals_:
            copy.wait()

        @pl.when(g < groups - 1)
        def _():
            far_copy().start()

    def queries_ready():
        for j in (1, 2, 3):
            arrived(token_rows(q_out, peers[j]), q_recv.at[peers[j]])

        @pl.when(g > 0)
        def _():
            arrived(kv_out.at[:, pl.ds(0, span)], far_recv)

    @pl.when(core == 0)
    def _():
        for ch in range(PARTS):
            forward(0, ch)
        keys_ready()
        og_relay(other, l, 0)
        for ch in range(PARTS):
            forward(1, ch)
        og_relay(other, l, 1)
        og_relay(t, y_l, 1)
        for ch in range(PARTS):
            forward(2, ch)
        queries_ready()
        for i in range(GROUP):
            softmax_block(i)
        og_relay(t, y_l, 0)
        og_relay(other, y_l, 1)
        og_relay(other, y_l, 0)

    @pl.when(core == 1)
    def _():
        keys_ready()

        @pl.when(g < groups - 1)
        def _():
            far_copy().wait_send()

        own_send(0)
        forward(0, 0)
        og_relay(other, l, 0)
        og_relay(other, l, 1)
        og_relay(t, y_l, 1)
        forward(1, 0)
        own_send(1)
        forward(0, 1)
        queries_ready()
        for i in range(GROUP):
            softmax_block(i)
        forward(2, 0)
        og_relay(t, y_l, 0)
        forward(1, 1)
        og_relay(other, y_l, 1)
        og_relay(other, y_l, 0)
        forward(2, 1)

    og_last()
    sums[...] = jnp.zeros_like(sums)

    def rows_of(ref, i):
        return ref.at[pl.ds(pl.multiple_of(i * rows, rows), rows)]

    def dq_target(member, ch):
        first, count = CHUNKS[ch]
        return q_grad.at[:, pl.ds(pl.multiple_of(member * wide + first * HD, HD), count * HD)]

    def dq_rows(i, ch):
        return dq.at[pl.ds(pl.multiple_of(i * rows, rows), rows), lanes_of(ch)]

    def dq_copy(i, ch):
        return send(dq_rows(i, ch), dq_target(l, ch), dq_send.at[i * PARTS + ch],
                    dq_recv.at[l * PARTS + ch], (base + i, t))

    def dq_stay(i, ch):
        return pltpu.make_async_copy(dq_rows(i, ch), dq_target(l, ch), home_sem.at[1 + ch])

    def part_of(ref, i):
        return ref.at[:, pl.ds(pl.multiple_of(i * rows, rows), rows)]

    def back_copy(i):
        return send(part_of(back, i), returned.at[l], back_send.at[i], back_recv.at[l],
                    (base - GROUP + i, t))

    def backward(ch):
        first_head, count = CHUNKS[ch]
        last = ch == PARTS - 1

        @pl.loop(0, GROUP)
        def _(i):
            r0 = pl.multiple_of(i * rows, rows)
            part, keys = pl.ds(r0, rows), pl.ds(r0, window)
            vw = kv_out[1, keys]
            dk = dv = 0.0
            for h in range(first_head, first_head + count):
                lanes = pl.ds(h * HD, HD)
                qh, gh = q_out[part, lanes], head_grad[part, lanes]
                prob_bf = stash[i * heads + h]
                delta = jnp.sum(attn[i * heads + h] * gh.T.astype(jnp.float32), axis=0, keepdims=True)
                dprob = dot(vw, gh, (1, 1))
                dscore = (prob_bf.astype(jnp.float32) * (dprob - delta)).astype(jnp.bfloat16)
                stash[i * heads + h] = dscore
                dk = dk + dot(dscore, qh, (1, 0))
                dv = dv + dot(prob_bf, gh, (1, 0))
            sums[0, keys] += dk
            sums[1, keys] += dv

            if last:
                @pl.when(g > 0)
                def _():
                    back[0, part] = (sums[0, part] * scaling).astype(back.dtype)
                    back[1, part] = sums[1, part].astype(back.dtype)
                    back_copy(i).start()

        if last:
            final[0] = (sums[0, span:] * scaling).astype(final.dtype)
            final[1] = sums[1, span:].astype(final.dtype)
            for i in range(GROUP):
                @pl.when(i != l)
                def _():
                    fin_copy(i).start()

                @pl.when(i == l)
                def _():
                    fin_stay(i).start()

        @pl.loop(0, GROUP)
        def _(i):
            r0 = pl.multiple_of(i * rows, rows)
            part, keys = pl.ds(r0, rows), pl.ds(r0, window)
            kw_t = kv_out[0, keys].T
            for h in range(first_head, first_head + count):
                grad = dot(kw_t, stash[i * heads + h], (1, 0)).T * scaling
                dq[part, pl.ds(h * HD, HD)] = grad.astype(dq.dtype)

            @pl.when(i != l)
            def _():
                dq_copy(i, ch).start()

            @pl.when(i == l)
            def _():
                dq_stay(i, ch).start()

    def fin_copy(i):
        return send(part_of(final, i), owned.at[l], fin_send.at[i], fin_recv.at[l], (base + i, t))

    def fin_stay(i):
        return pltpu.make_async_copy(part_of(final, i), owned.at[l], home_sem.at[0])

    for ch in range(PARTS):
        last = ch == PARTS - 1
        for step in range(1, groups - 1):
            collect(step, ch)
        if last:
            project(ch, early_slabs, True, False)
        collect(groups - 1, ch)
        if last:
            project(ch, [last_slab], False, True)
        else:
            project(ch, early_slabs + [last_slab], True, True)
        backward(ch)

    for j in (1, 2, 3):
        for ch in range(PARTS):
            arrived(dq_target(peers[j], ch), dq_recv.at[peers[j] * PARTS + ch])
        arrived(owned.at[peers[j]], fin_recv.at[peers[j]])
    fin_stay(l).wait()

    @pl.when(g < groups - 1)
    def _():
        for member in range(GROUP):
            arrived(returned.at[member], back_recv.at[member])

    for which, out in ((0, k_grad), (1, v_grad)):
        for member in range(GROUP):
            lanes = pl.ds(member * HD, HD)

            @pl.when(g < groups - 1)
            def _():
                out[:, lanes] = (owned[member, which].astype(jnp.float32)
                                 + returned[member, which].astype(jnp.float32)).astype(out.dtype)

            @pl.when(g == groups - 1)
            def _():
                out[:, lanes] = owned[member, which]

    for i in range(GROUP):
        @pl.when(i != l)
        def _():
            for ch in range(PARTS):
                dq_copy(i, ch).wait_send()
            fin_copy(i).wait_send()

        @pl.when(i == l)
        def _():
            for ch in range(PARTS):
                dq_stay(i, ch).wait()

        @pl.when(g > 0)
        def _():
            back_copy(i).wait_send()
    for arrival in og_arrivals:
        for copy in og_onward(*arrival):
            copy.wait_send()
    for copy in sends:
        copy.wait_send()

    @pl.when((g < groups - 1) & (core == 0))
    def _():
        far_copy().wait_send()

    @pl.when(g < groups - 1)
    def _():
        for step in range(groups):
            @pl.when(g >= step)
            def _():
                for j in range(GROUP):
                    for ch in range(PARTS):
                        up_copy(slab_piece(g - step, peers[j], ch), g - step, peers[j],
                                step, j, ch).wait_send()

    @pl.when(g > 0)
    def _():
        for step in range(groups):
            @pl.when(g + step < groups)
            def _():
                for j in range(GROUP):
                    for ch in range(PARTS):
                        down_copy(slab_piece(g + step, peers[j], ch), g + step, peers[j],
                                  step, j, ch).wait_send()


def store_kernel(*refs):
    count = (len(refs) - 2) // 3
    sources, targets, buffers = refs[:count], refs[count:2 * count], refs[2 * count:3 * count]
    come, leave = refs[-2:]
    copies = []
    for i in range(count):
        rows = sources[i].shape[0] // STORE_PARTS
        for j in range(STORE_PARTS):
            part, index = pl.ds(j * rows, rows), i * STORE_PARTS + j
            copies.append((
                pltpu.make_async_copy(sources[i].at[part], buffers[i].at[part], come.at[index]),
                pltpu.make_async_copy(buffers[i].at[part], targets[i].at[part], leave.at[index]),
            ))
    for inward, _ in copies:
        inward.start()
    for inward, outward in copies:
        inward.wait()
        outward.start()
    for _, outward in copies:
        outward.wait()


def grouped(q_proj, k_proj, v_proj, out_grad, o_weight, doc_extra):
    rows, width = q_proj.shape
    groups = lax.axis_size("ctx") // GROUP
    span, wide = GROUP * rows, width // GROUP
    depth, unit = o_weight.shape[0], out_grad.shape[1] // 2
    hbm = pl.BlockSpec(memory_space=pltpu.HBM)
    vmem = pl.BlockSpec(memory_space=pltpu.VMEM)
    bf16, f32, dma = jnp.bfloat16, jnp.float32, pltpu.SemaphoreType.DMA
    line = groups * GROUP
    grads = pl.pallas_call(
        functools.partial(step_kernel, groups, rows),
        out_shape=(
            jax.ShapeDtypeStruct((rows, width), bf16),
            jax.ShapeDtypeStruct((rows, GROUP * HD), bf16),
            jax.ShapeDtypeStruct((rows, GROUP * HD), bf16),
        ),
        in_specs=[hbm] * 5 + [pl.BlockSpec(memory_space=pltpu.SMEM)],
        out_specs=(vmem, vmem, vmem),
        scratch_shapes=[
            pltpu.VMEM((groups, span, unit), bf16),
            [pltpu.VMEM((groups, GROUP * depth, count * HD), bf16) for _, count in CHUNKS],
            pltpu.VMEM((span, wide), f32),
            pltpu.VMEM((span, wide), bf16),
            pltpu.VMEM((span, wide), bf16),
            pltpu.VMEM((2, 2 * span, HD), bf16),
            pltpu.VMEM((GROUP * wide // HD, (GROUP + 1) * rows, rows), bf16),
            pltpu.VMEM((GROUP * wide // HD, HD, rows), f32),
            pltpu.VMEM((2, 2 * span, HD), f32),
            pltpu.VMEM((span, wide), bf16),
            pltpu.VMEM((2, span, HD), bf16),
            pltpu.VMEM((GROUP, 2, rows, HD), bf16),
            pltpu.VMEM((2, span, HD), bf16),
            pltpu.VMEM((GROUP, 2, rows, HD), bf16),
            dma((5 + PARTS,)), dma((3 * PARTS,)), dma((line * PARTS,)), dma((line * PARTS,)), dma((line * PARTS,)),
            dma((14,)), dma((4 * GROUP,)), dma((3,)), dma((GROUP,)),
            dma((6,)), dma((2 * GROUP,)), dma, dma,
            dma((GROUP * PARTS,)), dma((GROUP * PARTS,)), dma((GROUP,)), dma((GROUP,)),
            dma((GROUP,)), dma((GROUP,)), dma((1 + PARTS,)),
        ],
        compiler_params=pltpu.CompilerParams(
            collective_id=0, has_side_effects=True, vmem_limit_bytes=56 << 20),
    )(q_proj, k_proj, v_proj, out_grad, o_weight, doc_extra)
    return pl.pallas_call(
        store_kernel,
        out_shape=tuple(jax.ShapeDtypeStruct(grad.shape, grad.dtype) for grad in grads),
        in_specs=[pl.BlockSpec(memory_space=pl.ANY)] * 3,
        out_specs=(hbm, hbm, hbm),
        scratch_shapes=[pltpu.VMEM(grad.shape, grad.dtype) for grad in grads] + [dma((3 * STORE_PARTS,))] * 2,
    )(*grads)


def fits(mesh):
    ctx, tp = mesh.shape["ctx"], mesh.shape["tp"]
    return tp == 2 and ctx == 4 * GROUP and KVH // tp == GROUP


def solution(mesh):
    placed = (P("ctx", "tp"), P("ctx", "tp"), P("ctx", "tp"), P("ctx", "tp"), P("ctx", "tp"), P())
    return jax.shard_map(
        grouped if fits(mesh) else local,
        mesh=mesh,
        in_specs=placed,
        out_specs=(P("ctx", "tp"), P("ctx", "tp"), P("ctx", "tp")),
        check_vma=False,
    )
```

```python
import functools
import math

import jax
import jax.numpy as jnp
from jax import lax
from jax.experimental import pallas as pl
from jax.experimental.pallas import tpu as pltpu
from jax.sharding import PartitionSpec as P

H = 32
KVH = 8
HD = 128
DOC_MIN = 256
DOC_MAX = 1024


NEG_FILL = -1e30


def shifted(value, axis, steps):
    count = lax.axis_size(axis)
    leading, last = (max(0, -steps), min(count, count - steps))
    return lax.ppermute(value, axis, [(source, source + steps) for source in range(leading, last)])


def keep_state(state):
    return state


def local(q_proj, k_proj, v_proj, out_grad, o_weight, doc_extra):
    tok_rows = q_proj.shape[0]
    kv_local = k_proj.shape[1] // HD
    q_group = H // KVH
    scaling = 1.0 / math.sqrt(HD)
    reach = DOC_MAX // tok_rows
    dev_index = lax.axis_index("ctx")
    gathered = lax.all_gather(out_grad, "tp", axis=1, tiled=True)
    head_sum = jnp.dot(
        gathered,
        lax.all_gather(o_weight, "ctx", axis=0, tiled=True),
        preferred_element_type=jnp.float32,
    )
    head_grad = head_sum.astype(jnp.bfloat16).reshape(tok_rows, kv_local, q_group, HD)
    queries = q_proj.reshape(tok_rows, kv_local, q_group, HD)
    order = jnp.arange(doc_extra.shape[0], dtype=jnp.int32)
    earlier = order[:, None] > order[None, :]
    doc_starts = jnp.sum(jnp.where(earlier, DOC_MIN + doc_extra[None, :], 0), axis=1)
    position = dev_index * tok_rows + jnp.arange(tok_rows, dtype=jnp.int32)
    doc_first = jnp.max(
        jnp.where(doc_starts[None, :] <= position[:, None], doc_starts[None, :], 0), axis=1
    )
    stacked = jnp.stack([k_proj, v_proj])
    sources = [stacked]
    moving = stacked
    for offset in range(1, reach + 1):
        moving = shifted(moving, "ctx", 1)
        sources.append(moving)

    def scores_for(source, offset):
        key_block = source[0].reshape(tok_rows, kv_local, HD)
        raw_scores = (
            jnp.einsum("tgqd,kgd->gqtk", queries, key_block, preferred_element_type=jnp.float32)
            * scaling
        )
        key_pos = (dev_index - offset) * tok_rows + jnp.arange(tok_rows, dtype=jnp.int32)
        allowed = (key_pos[None, :] >= doc_first[:, None]) & (key_pos[None, :] <= position[:, None])
        return (raw_scores, allowed)

    def is_live(offset):
        return (dev_index - offset >= 0) & (doc_first[0] <= (dev_index - offset + 1) * tok_rows - 1)

    raw_scores, allowed = scores_for(sources[0], 0)
    masked = jnp.where(allowed, raw_scores, NEG_FILL)
    row_peak = jnp.max(masked, axis=-1)
    row_total = jnp.sum(jnp.exp(masked - row_peak[..., None]), axis=-1)
    for offset in range(1, reach + 1):

        def merge_block(state):
            old_peak, old_total = state
            scores_new, allowed_new = scores_for(sources[offset], offset)
            masked_new = jnp.where(allowed_new, scores_new, NEG_FILL)
            new_peak = jnp.maximum(old_peak, jnp.max(masked_new, axis=-1))
            new_total = old_total * jnp.exp(old_peak - new_peak) + jnp.sum(
                jnp.exp(masked_new - new_peak[..., None]), axis=-1
            )
            return (new_peak, new_total)

        row_peak, row_total = lax.cond(
            is_live(offset), merge_block, keep_state, (row_peak, row_total)
        )
    log_total = row_peak + jnp.log(row_total)

    def soft_weights(source, offset):
        scores_here, allowed_here = scores_for(source, offset)
        return jnp.where(allowed_here, jnp.exp(scores_here - log_total[..., None]), 0.0)

    def add_output(running, source, offset):
        soft_bf = soft_weights(source, offset).astype(jnp.bfloat16)
        val_block = source[1].reshape(tok_rows, kv_local, HD)
        return running + jnp.einsum(
            "gqtk,kgd->gqtd", soft_bf, val_block, preferred_element_type=jnp.float32
        )

    attn_out = add_output(jnp.zeros((kv_local, q_group, tok_rows, HD), jnp.float32), sources[0], 0)
    for offset in range(1, reach + 1):

        def add_live(running):
            return add_output(running, sources[offset], offset)

        attn_out = lax.cond(is_live(offset), add_live, keep_state, attn_out)
    delta = jnp.sum(head_grad.transpose(1, 2, 0, 3).astype(jnp.float32) * attn_out, axis=-1)

    def grads_for(source, offset):
        key_block = source[0].reshape(tok_rows, kv_local, HD)
        val_block = source[1].reshape(tok_rows, kv_local, HD)
        soft = soft_weights(source, offset)
        soft_bf = soft.astype(jnp.bfloat16)
        dprob = jnp.einsum(
            "tgqd,kgd->gqtk", head_grad, val_block, preferred_element_type=jnp.float32
        )
        dscore = (soft * (dprob - delta[..., None])).astype(jnp.bfloat16)
        q_part = jnp.einsum("gqtk,kgd->tgqd", dscore, key_block, preferred_element_type=jnp.float32)
        k_part = (
            jnp.einsum("gqtk,tgqd->kgd", dscore, queries, preferred_element_type=jnp.float32)
            * scaling
        )
        v_part = jnp.einsum(
            "gqtk,tgqd->kgd", soft_bf, head_grad, preferred_element_type=jnp.float32
        )
        return (q_part, k_part, v_part)

    q_acc, k_acc, v_acc = grads_for(sources[0], 0)
    for offset in range(1, reach + 1):

        def live_grads(unused):
            return grads_for(sources[offset], offset)

        def no_grads(unused):
            return (jnp.zeros_like(q_acc), jnp.zeros_like(k_acc), jnp.zeros_like(v_acc))

        q_add, k_add, v_add = lax.cond(is_live(offset), live_grads, no_grads, 0)
        q_acc = q_acc + q_add
        sent = jnp.stack([k_add, v_add]).astype(jnp.bfloat16).reshape(2, tok_rows, kv_local * HD)
        returned = shifted(sent, "ctx", -offset)
        k_acc = k_acc + returned[0].astype(jnp.float32).reshape(tok_rows, kv_local, HD)
        v_acc = v_acc + returned[1].astype(jnp.float32).reshape(tok_rows, kv_local, HD)
    q_grad = (q_acc * scaling).astype(jnp.bfloat16).reshape(tok_rows, kv_local * q_group * HD)
    k_grad = k_acc.astype(jnp.bfloat16).reshape(tok_rows, kv_local * HD)
    v_grad = v_acc.astype(jnp.bfloat16).reshape(tok_rows, kv_local * HD)
    return (q_grad, k_grad, v_grad)


GROUP = 4
STORE_PARTS = 4
PARTS = 2
MESH = pl.DeviceIdType.MESH


def place():
    me, t = lax.axis_index("ctx"), lax.axis_index("tp")
    return me, t, me // GROUP, me % GROUP


def send(src, dst, send_sem, recv_sem, device):
    return pltpu.make_async_remote_copy(
        src_ref=src, dst_ref=dst, send_sem=send_sem, recv_sem=recv_sem,
        device_id=device, device_id_type=MESH,
    )


def arrived(ref, sem):
    pltpu.make_async_copy(ref, ref, sem).wait()


def greet(devices, groups, g, t):
    barrier = pltpu.get_barrier_semaphore()

    def signal(device):
        pl.semaphore_signal(barrier, inc=1, device_id=device, device_id_type=MESH)

    for device in devices:
        signal(device)

    @pl.when(g > 0)
    def _():
        for member in range(GROUP):
            signal(((g - 1) * GROUP + member, t))

    @pl.when(g < groups - 1)
    def _():
        for member in range(GROUP):
            signal(((g + 1) * GROUP + member, t))

    inner = jnp.where((g > 0) & (g < groups - 1), GROUP, 0)
    pl.semaphore_wait(barrier, len(devices) + GROUP + inner)


def step_kernel(
    groups, rows, q, k, v, og, w, extra, q_grad, k_grad, v_grad,
    ogb, wb, acc, head_grad, q_out, kv_out, stash, attn, sums, dq, back, returned, final, owned,
    local_sem, w_send, w_recv, up_send, down_send, og_send, og_recv, q_send, q_recv,
    kv_send, kv_recv, far_send, far_recv,
    dq_send, dq_recv, back_send, back_recv, fin_send, fin_recv, home_sem,
):
    me, t, g, l = place()
    base = g * GROUP
    wide, span = q.shape[1] // GROUP, GROUP * rows
    depth = w.shape[0]
    unit = ogb.shape[2]
    x_dev, y_l, c_l = (me, 1 - t), (l + 2) % GROUP, l + 1 - 2 * (l % 2)
    core = l % 2
    far_chip = 2 - 2 * (l // 2)
    peers = [l, c_l, far_chip, far_chip + 1]
    y_dev, c_dev = (base + y_l, t), (base + c_l, t)
    above, below = (me + GROUP, t), (me - GROUP, t)
    greet([(base + peers[j], t) for j in (1, 2, 3)] + [x_dev], groups, g, t)

    def cols(ref, index, size):
        return ref.at[:, pl.ds(pl.multiple_of(index * size, size), size)]

    narrow = wide // PARTS

    def lanes_of(ch):
        return pl.ds(pl.multiple_of(ch * narrow, HD), narrow)

    def slab_piece(group, member, ch):
        return wb.at[ch, group, pl.ds(pl.multiple_of(member * depth, depth), depth)]

    def w_cols(member, ch):
        return w.at[:, pl.ds(pl.multiple_of(member * wide + ch * narrow, HD), narrow)]

    def w_sem(group, member, ch):
        return w_recv.at[(group * GROUP + member) * PARTS + ch]

    def token_rows(ref, member):
        return ref.at[pl.ds(pl.multiple_of(member * rows, rows), rows)]

    def og_unit(tt, member, u):
        return ogb.at[tt * 2 + u, pl.ds(pl.multiple_of(member * rows, rows), rows)]

    def og_own(u):
        return og.at[:, pl.ds(u * unit, unit)]

    def og_sem(tt, member, u):
        return og_recv.at[(tt * GROUP + member) * 2 + u]

    def kv_rows(which, member):
        return kv_out.at[which, pl.ds(pl.multiple_of(span + member * rows, rows), rows)]

    sends, locals_ = [], []

    def go(copy):
        copy.start()
        sends.append(copy)

    def stay(src, dst):
        copy = pltpu.make_async_copy(src, dst, local_sem.at[len(locals_)])
        copy.start()
        locals_.append(copy)

    def up_copy(src, group, member, step, j, ch):
        return send(src, slab_piece(group, member, ch), up_send.at[(step * GROUP + j) * PARTS + ch],
                    w_sem(group, member, ch), above)

    def down_copy(src, group, member, step, j, ch):
        return send(src, slab_piece(group, member, ch), down_send.at[(step * GROUP + j) * PARTS + ch],
                    w_sem(group, member, ch), below)

    def own_send(ch):
        @pl.when(g < groups - 1)
        def _():
            up_copy(w_cols(l, ch), g, l, 0, 0, ch).start()

        @pl.when(g > 0)
        def _():
            down_copy(w_cols(l, ch), g, l, 0, 0, ch).start()

    @pl.when(core == 0)
    def _():
        for ch in range(PARTS):
            own_send(ch)

    def w_to(j):
        for ch in range(PARTS):
            go(send(w_cols(peers[j], ch), slab_piece(g, l, ch), w_send.at[(j - 1) * PARTS + ch],
                    w_sem(g, l, ch), (base + peers[j], t)))

    w_to(2)
    w_to(1)
    for which, ref in ((0, k), (1, v)):
        for j in (1, 2, 3):
            go(send(cols(ref, peers[j], HD), kv_rows(which, l), kv_send.at[which * 3 + j - 1],
                    kv_recv.at[which * GROUP + l], (base + peers[j], t)))
        stay(cols(ref, l, HD), kv_rows(which, l))
    w_to(3)
    for u in (0, 1):
        go(send(og_own(u), og_unit(t, l, u), og_send.at[u], og_sem(t, l, u), x_dev))
    for ch in range(PARTS):
        stay(w_cols(l, ch), slab_piece(g, l, ch))
    for u in (0, 1):
        go(send(og_own(u), og_unit(t, l, u), og_send.at[4 + u], og_sem(t, l, u), c_dev))
        stay(og_own(u), og_unit(t, l, u))
    for u in (1, 0):
        go(send(og_own(u), og_unit(t, l, u), og_send.at[2 + u], og_sem(t, l, u), y_dev))
    for j in (1, 2, 3):
        go(send(cols(q, peers[j], wide), token_rows(q_out, l), q_send.at[j - 1],
                q_recv.at[l], (base + peers[j], t)))
    stay(cols(q, l, wide), token_rows(q_out, l))

    @pl.when(g == 0)
    def _():
        kv_out[:, 0:span] = jnp.zeros((2, span, HD), kv_out.dtype)

    sums[...] = jnp.zeros_like(sums)

    def forward(step, ch):
        if step == 0:
            for j in range(1, GROUP):
                piece = slab_piece(g, peers[j], ch)
                arrived(piece, w_sem(g, peers[j], ch))

                @pl.when(g < groups - 1)
                def _():
                    up_copy(piece, g, peers[j], 0, j, ch).start()

                @pl.when(g > 0)
                def _():
                    down_copy(piece, g, peers[j], 0, j, ch).start()
        else:
            for j in range(GROUP):
                @pl.when((g >= step) & (g < groups - 1))
                def _():
                    piece = slab_piece(g - step, peers[j], ch)
                    arrived(piece, w_sem(g - step, peers[j], ch))
                    up_copy(piece, g - step, peers[j], step, j, ch).start()

                @pl.when((g + step < groups) & (g > 0))
                def _():
                    piece = slab_piece(g + step, peers[j], ch)
                    arrived(piece, w_sem(g + step, peers[j], ch))
                    down_copy(piece, g + step, peers[j], step, j, ch).start()

    def collect(step, ch):
        @pl.when((g >= step) & (g == groups - 1))
        def _():
            for j in range(GROUP):
                arrived(slab_piece(g - step, peers[j], ch), w_sem(g - step, peers[j], ch))

        @pl.when((g + step < groups) & (g == 0))
        def _():
            for j in range(GROUP):
                arrived(slab_piece(g + step, peers[j], ch), w_sem(g + step, peers[j], ch))

    last_slab = jnp.where(2 * g < groups, groups - 1, 0)
    early_slabs = [(last_slab + 1 + n) % groups for n in range(groups - 1)]

    def project(ch, terms, finish):
        lanes = lanes_of(ch)

        @pl.loop(0, GROUP)
        def _(i):
            part = pl.ds(pl.multiple_of(i * rows, rows), rows)
            total = acc[part] if finish else 0.0
            for slab in terms:
                total = total + jnp.dot(
                    ogb[slab, part], wb[ch, slab], preferred_element_type=jnp.float32)
            if finish:
                head_grad[part, lanes] = total.astype(head_grad.dtype)
            else:
                acc[part] = total

    def og_pass(tt, member, u, index, device):
        return send(og_unit(tt, member, u), og_unit(tt, member, u), og_send.at[index],
                    og_sem(tt, member, u), device)

    def og_onward(tt, member, u):
        if tt is not t:
            return [og_pass(tt, member, u, (8 if member is l else 12) + u, c_dev)]
        return [og_pass(tt, member, u, 6 + u, x_dev), og_pass(tt, member, u, 10 + u, c_dev)]

    other = 1 - t
    og_arrivals = [(tt, member, u) for tt, member in ((other, l), (t, y_l), (other, y_l))
                   for u in (0, 1)]

    def og_relay(tt, member, u):
        arrived(og_unit(tt, member, u), og_sem(tt, member, u))
        for copy in og_onward(tt, member, u):
            copy.start()

    def og_last():
        for member in (c_l, (c_l + 2) % GROUP):
            for tt in (t, 1 - t):
                for u in (0, 1):
                    arrived(og_unit(tt, member, u), og_sem(tt, member, u))

    def far_copy():
        return send(kv_out.at[:, pl.ds(span, span)], kv_out.at[:, pl.ds(0, span)],
                    far_send, far_recv, above)

    window = (GROUP + 1) * rows
    heads = wide // HD
    scaling = 1.0 / math.sqrt(HD)
    column = lax.broadcasted_iota(jnp.int32, (window, rows), 0)
    row = lax.broadcasted_iota(jnp.int32, (window, rows), 1)
    causal = column <= span + row
    lane = lax.broadcasted_iota(jnp.int32, (1, rows), 1)

    def first_of(i):
        position = g * span + i * rows + lane
        start, found = jnp.int32(0), jnp.zeros((1, rows), jnp.int32)
        for j in range(extra.shape[0]):
            found = jnp.where(position >= start, start, found)
            start = start + DOC_MIN + extra[j]
        return found

    def dot(a, b, dims):
        return lax.dot_general(a, b, ((dims[:1], dims[1:]), ((), ())),
                               preferred_element_type=jnp.float32)

    def softmax_block(i):
        r0 = pl.multiple_of(i * rows, rows)
        part, keys = pl.ds(r0, rows), pl.ds(r0, window)
        kw = kv_out[0, keys]
        vw_t = kv_out[1, keys].T
        allowed = causal & (column >= first_of(i) - ((g - 1) * span + i * rows))

        for h in range(heads):
            score = jnp.where(allowed, dot(kw, q_out[part, pl.ds(h * HD, HD)], (1, 1)), NEG_FILL)
            expd = jnp.exp((score - jnp.max(score, axis=0, keepdims=True)) * scaling)
            prob = expd * (1.0 / jnp.sum(expd, axis=0, keepdims=True))
            prob_bf = prob.astype(stash.dtype)
            stash[i * heads + h] = prob_bf
            attn[i * heads + h] = dot(vw_t, prob_bf, (1, 0))

    def keys_ready():
        for which in (0, 1):
            for j in (1, 2, 3):
                arrived(kv_rows(which, peers[j]), kv_recv.at[which * GROUP + peers[j]])
        for copy in locals_:
            copy.wait()

        @pl.when(g < groups - 1)
        def _():
            far_copy().start()

    def queries_ready():
        for j in (1, 2, 3):
            arrived(token_rows(q_out, peers[j]), q_recv.at[peers[j]])

        @pl.when(g > 0)
        def _():
            arrived(kv_out.at[:, pl.ds(0, span)], far_recv)

    @pl.when(core == 0)
    def _():
        for ch in range(PARTS):
            forward(0, ch)
        keys_ready()
        og_relay(other, l, 0)
        for ch in range(PARTS):
            forward(1, ch)
        og_relay(t, y_l, 1)
        og_relay(other, l, 1)
        og_relay(t, y_l, 0)
        for ch in range(PARTS):
            forward(2, ch)
        og_relay(other, y_l, 1)

    @pl.when(core == 1)
    def _():
        keys_ready()
        og_relay(other, l, 0)

        @pl.when(g < groups - 1)
        def _():
            far_copy().wait_send()

        own_send(0)
        forward(0, 0)
        og_relay(t, y_l, 1)
        og_relay(other, l, 1)
        own_send(1)
        forward(0, 1)
        og_relay(t, y_l, 0)
        og_relay(other, y_l, 1)
        forward(1, 0)
        forward(2, 0)
        forward(1, 1)

    queries_ready()

    @pl.loop(0, GROUP)
    def _(i):
        softmax_block(i)

        @pl.when((core == 1) & (i == 1))
        def _():
            forward(2, 1)

        @pl.when(i == 0)
        def _():
            og_relay(other, y_l, 0)

    og_last()
    sums[...] = jnp.zeros_like(sums)

    def rows_of(ref, i):
        return ref.at[pl.ds(pl.multiple_of(i * rows, rows), rows)]

    def dq_target(member, ch):
        return q_grad.at[:, pl.ds(pl.multiple_of(member * wide + ch * narrow, HD), narrow)]

    def dq_rows(i, ch):
        return dq.at[pl.ds(pl.multiple_of(i * rows, rows), rows), lanes_of(ch)]

    def dq_copy(i, ch):
        return send(dq_rows(i, ch), dq_target(l, ch), dq_send.at[i * PARTS + ch],
                    dq_recv.at[l * PARTS + ch], (base + i, t))

    def dq_stay(i, ch):
        return pltpu.make_async_copy(dq_rows(i, ch), dq_target(l, ch), home_sem.at[1 + ch])

    def part_of(ref, i):
        return ref.at[:, pl.ds(pl.multiple_of(i * rows, rows), rows)]

    def back_copy(i):
        return send(part_of(back, i), returned.at[l], back_send.at[i], back_recv.at[l],
                    (base - GROUP + i, t))

    def backward(ch):
        last = ch == PARTS - 1
        count = heads // PARTS

        @pl.loop(0, GROUP)
        def _(i):
            r0 = pl.multiple_of(i * rows, rows)
            part, keys = pl.ds(r0, rows), pl.ds(r0, window)
            vw = kv_out[1, keys]
            dk = dv = 0.0
            for n in range(count):
                h = ch * count + n
                lanes = pl.ds(pl.multiple_of(h * HD, HD), HD)
                qh, gh = q_out[part, lanes], head_grad[part, lanes]
                prob_bf = stash[i * heads + h]
                delta = jnp.sum(attn[i * heads + h] * gh.T.astype(jnp.float32), axis=0, keepdims=True)
                dprob = dot(vw, gh, (1, 1))
                dscore = (prob_bf.astype(jnp.float32) * (dprob - delta)).astype(jnp.bfloat16)
                stash[i * heads + h] = dscore
                dk = dk + dot(dscore, qh, (1, 0))
                dv = dv + dot(prob_bf, gh, (1, 0))
            sums[0, keys] += dk
            sums[1, keys] += dv

            @pl.when(last & (g > 0))
            def _():
                back[0, part] = (sums[0, part] * scaling).astype(back.dtype)
                back[1, part] = sums[1, part].astype(back.dtype)
                back_copy(i).start()

        @pl.when(last)
        def _():
            final[0] = (sums[0, span:] * scaling).astype(final.dtype)
            final[1] = sums[1, span:].astype(final.dtype)
            for i in range(GROUP):
                @pl.when(i != l)
                def _():
                    fin_copy(i).start()

                @pl.when(i == l)
                def _():
                    fin_stay(i).start()

        @pl.loop(0, GROUP)
        def _(i):
            r0 = pl.multiple_of(i * rows, rows)
            part, keys = pl.ds(r0, rows), pl.ds(r0, window)
            kw_t = kv_out[0, keys].T
            for n in range(count):
                h = ch * count + n
                grad = dot(kw_t, stash[i * heads + h], (1, 0)).T * scaling
                dq[part, pl.ds(pl.multiple_of(h * HD, HD), HD)] = grad.astype(dq.dtype)

            @pl.when(i != l)
            def _():
                dq_copy(i, ch).start()

            @pl.when(i == l)
            def _():
                dq_stay(i, ch).start()

    def fin_copy(i):
        return send(part_of(final, i), owned.at[l], fin_send.at[i], fin_recv.at[l], (base + i, t))

    def fin_stay(i):
        return pltpu.make_async_copy(part_of(final, i), owned.at[l], home_sem.at[0])

    @pl.loop(0, PARTS)
    def _(ch):
        for step in range(1, groups - 1):
            collect(step, ch)
        project(ch, early_slabs, False)
        collect(groups - 1, ch)
        project(ch, [last_slab], True)
        backward(ch)

    for j in (1, 2, 3):
        for ch in range(PARTS):
            arrived(dq_target(peers[j], ch), dq_recv.at[peers[j] * PARTS + ch])
        arrived(owned.at[peers[j]], fin_recv.at[peers[j]])
    fin_stay(l).wait()

    @pl.when(g < groups - 1)
    def _():
        for member in range(GROUP):
            arrived(returned.at[member], back_recv.at[member])

    for which, out in ((0, k_grad), (1, v_grad)):
        for member in range(GROUP):
            lanes = pl.ds(member * HD, HD)

            @pl.when(g < groups - 1)
            def _():
                out[:, lanes] = (owned[member, which].astype(jnp.float32)
                                 + returned[member, which].astype(jnp.float32)).astype(out.dtype)

            @pl.when(g == groups - 1)
            def _():
                out[:, lanes] = owned[member, which]

    for i in range(GROUP):
        @pl.when(i != l)
        def _():
            for ch in range(PARTS):
                dq_copy(i, ch).wait_send()
            fin_copy(i).wait_send()

        @pl.when(i == l)
        def _():
            for ch in range(PARTS):
                dq_stay(i, ch).wait()

        @pl.when(g > 0)
        def _():
            back_copy(i).wait_send()
    for arrival in og_arrivals:
        for copy in og_onward(*arrival):
            copy.wait_send()
    for copy in sends:
        copy.wait_send()

    @pl.when((g < groups - 1) & (core == 0))
    def _():
        far_copy().wait_send()

    @pl.when(g < groups - 1)
    def _():
        for step in range(groups):
            @pl.when(g >= step)
            def _():
                for j in range(GROUP):
                    for ch in range(PARTS):
                        up_copy(slab_piece(g - step, peers[j], ch), g - step, peers[j],
                                step, j, ch).wait_send()

    @pl.when(g > 0)
    def _():
        for step in range(groups):
            @pl.when(g + step < groups)
            def _():
                for j in range(GROUP):
                    for ch in range(PARTS):
                        down_copy(slab_piece(g + step, peers[j], ch), g + step, peers[j],
                                  step, j, ch).wait_send()


def store_kernel(*refs):
    count = (len(refs) - 2) // 3
    sources, targets, buffers = refs[:count], refs[count:2 * count], refs[2 * count:3 * count]
    come, leave = refs[-2:]
    copies = []
    for i in range(count):
        rows = sources[i].shape[0] // STORE_PARTS
        for j in range(STORE_PARTS):
            part, index = pl.ds(j * rows, rows), i * STORE_PARTS + j
            copies.append((
                pltpu.make_async_copy(sources[i].at[part], buffers[i].at[part], come.at[index]),
                pltpu.make_async_copy(buffers[i].at[part], targets[i].at[part], leave.at[index]),
            ))
    for inward, _ in copies:
        inward.start()
    for inward, outward in copies:
        inward.wait()
        outward.start()
    for _, outward in copies:
        outward.wait()


def grouped(q_proj, k_proj, v_proj, out_grad, o_weight, doc_extra):
    rows, width = q_proj.shape
    groups = lax.axis_size("ctx") // GROUP
    span, wide = GROUP * rows, width // GROUP
    depth, unit = o_weight.shape[0], out_grad.shape[1] // 2
    hbm = pl.BlockSpec(memory_space=pltpu.HBM)
    vmem = pl.BlockSpec(memory_space=pltpu.VMEM)
    bf16, f32, dma = jnp.bfloat16, jnp.float32, pltpu.SemaphoreType.DMA
    line = groups * GROUP
    grads = pl.pallas_call(
        functools.partial(step_kernel, groups, rows),
        out_shape=(
            jax.ShapeDtypeStruct((rows, width), bf16),
            jax.ShapeDtypeStruct((rows, GROUP * HD), bf16),
            jax.ShapeDtypeStruct((rows, GROUP * HD), bf16),
        ),
        in_specs=[hbm] * 5 + [pl.BlockSpec(memory_space=pltpu.SMEM)],
        out_specs=(vmem, vmem, vmem),
        scratch_shapes=[
            pltpu.VMEM((groups, span, unit), bf16),
            pltpu.VMEM((PARTS, groups, GROUP * depth, wide // PARTS), bf16),
            pltpu.VMEM((span, wide // PARTS), f32),
            pltpu.VMEM((span, wide), bf16),
            pltpu.VMEM((span, wide), bf16),
            pltpu.VMEM((2, 2 * span, HD), bf16),
            pltpu.VMEM((GROUP * wide // HD, (GROUP + 1) * rows, rows), bf16),
            pltpu.VMEM((GROUP * wide // HD, HD, rows), f32),
            pltpu.VMEM((2, 2 * span, HD), f32),
            pltpu.VMEM((span, wide), bf16),
            pltpu.VMEM((2, span, HD), bf16),
            pltpu.VMEM((GROUP, 2, rows, HD), bf16),
            pltpu.VMEM((2, span, HD), bf16),
            pltpu.VMEM((GROUP, 2, rows, HD), bf16),
            dma((5 + PARTS,)), dma((3 * PARTS,)), dma((line * PARTS,)), dma((line * PARTS,)), dma((line * PARTS,)),
            dma((14,)), dma((4 * GROUP,)), dma((3,)), dma((GROUP,)),
            dma((6,)), dma((2 * GROUP,)), dma, dma,
            dma((GROUP * PARTS,)), dma((GROUP * PARTS,)), dma((GROUP,)), dma((GROUP,)),
            dma((GROUP,)), dma((GROUP,)), dma((1 + PARTS,)),
        ],
        compiler_params=pltpu.CompilerParams(
            collective_id=0, has_side_effects=True, vmem_limit_bytes=56 << 20),
    )(q_proj, k_proj, v_proj, out_grad, o_weight, doc_extra)
    return pl.pallas_call(
        store_kernel,
        out_shape=tuple(jax.ShapeDtypeStruct(grad.shape, grad.dtype) for grad in grads),
        in_specs=[pl.BlockSpec(memory_space=pl.ANY)] * 3,
        out_specs=(hbm, hbm, hbm),
        scratch_shapes=[pltpu.VMEM(grad.shape, grad.dtype) for grad in grads] + [dma((3 * STORE_PARTS,))] * 2,
    )(*grads)


def fits(mesh):
    ctx, tp = mesh.shape["ctx"], mesh.shape["tp"]
    return tp == 2 and ctx == 4 * GROUP and KVH // tp == GROUP


def solution(mesh):
    placed = (P("ctx", "tp"), P("ctx", "tp"), P("ctx", "tp"), P("ctx", "tp"), P("ctx", "tp"), P())
    return jax.shard_map(
        grouped if fits(mesh) else local,
        mesh=mesh,
        in_specs=placed,
        out_specs=(P("ctx", "tp"), P("ctx", "tp"), P("ctx", "tp")),
        check_vma=False,
    )
```

```python
import functools
import math

import jax
import jax.numpy as jnp
from jax import lax
from jax.experimental import pallas as pl
from jax.experimental.pallas import tpu as pltpu
from jax.sharding import PartitionSpec as P

H = 32
KVH = 8
HD = 128
DOC_MIN = 256
DOC_MAX = 1024


NEG_FILL = -1e30


def shifted(value, axis, steps):
    count = lax.axis_size(axis)
    leading, last = (max(0, -steps), min(count, count - steps))
    return lax.ppermute(value, axis, [(source, source + steps) for source in range(leading, last)])


def keep_state(state):
    return state


def local(q_proj, k_proj, v_proj, out_grad, o_weight, doc_extra):
    tok_rows = q_proj.shape[0]
    kv_local = k_proj.shape[1] // HD
    q_group = H // KVH
    scaling = 1.0 / math.sqrt(HD)
    reach = DOC_MAX // tok_rows
    dev_index = lax.axis_index("ctx")
    gathered = lax.all_gather(out_grad, "tp", axis=1, tiled=True)
    head_sum = jnp.dot(
        gathered,
        lax.all_gather(o_weight, "ctx", axis=0, tiled=True),
        preferred_element_type=jnp.float32,
    )
    head_grad = head_sum.astype(jnp.bfloat16).reshape(tok_rows, kv_local, q_group, HD)
    queries = q_proj.reshape(tok_rows, kv_local, q_group, HD)
    order = jnp.arange(doc_extra.shape[0], dtype=jnp.int32)
    earlier = order[:, None] > order[None, :]
    doc_starts = jnp.sum(jnp.where(earlier, DOC_MIN + doc_extra[None, :], 0), axis=1)
    position = dev_index * tok_rows + jnp.arange(tok_rows, dtype=jnp.int32)
    doc_first = jnp.max(
        jnp.where(doc_starts[None, :] <= position[:, None], doc_starts[None, :], 0), axis=1
    )
    stacked = jnp.stack([k_proj, v_proj])
    sources = [stacked]
    moving = stacked
    for offset in range(1, reach + 1):
        moving = shifted(moving, "ctx", 1)
        sources.append(moving)

    def scores_for(source, offset):
        key_block = source[0].reshape(tok_rows, kv_local, HD)
        raw_scores = (
            jnp.einsum("tgqd,kgd->gqtk", queries, key_block, preferred_element_type=jnp.float32)
            * scaling
        )
        key_pos = (dev_index - offset) * tok_rows + jnp.arange(tok_rows, dtype=jnp.int32)
        allowed = (key_pos[None, :] >= doc_first[:, None]) & (key_pos[None, :] <= position[:, None])
        return (raw_scores, allowed)

    def is_live(offset):
        return (dev_index - offset >= 0) & (doc_first[0] <= (dev_index - offset + 1) * tok_rows - 1)

    raw_scores, allowed = scores_for(sources[0], 0)
    masked = jnp.where(allowed, raw_scores, NEG_FILL)
    row_peak = jnp.max(masked, axis=-1)
    row_total = jnp.sum(jnp.exp(masked - row_peak[..., None]), axis=-1)
    for offset in range(1, reach + 1):

        def merge_block(state):
            old_peak, old_total = state
            scores_new, allowed_new = scores_for(sources[offset], offset)
            masked_new = jnp.where(allowed_new, scores_new, NEG_FILL)
            new_peak = jnp.maximum(old_peak, jnp.max(masked_new, axis=-1))
            new_total = old_total * jnp.exp(old_peak - new_peak) + jnp.sum(
                jnp.exp(masked_new - new_peak[..., None]), axis=-1
            )
            return (new_peak, new_total)

        row_peak, row_total = lax.cond(
            is_live(offset), merge_block, keep_state, (row_peak, row_total)
        )
    log_total = row_peak + jnp.log(row_total)

    def soft_weights(source, offset):
        scores_here, allowed_here = scores_for(source, offset)
        return jnp.where(allowed_here, jnp.exp(scores_here - log_total[..., None]), 0.0)

    def add_output(running, source, offset):
        soft_bf = soft_weights(source, offset).astype(jnp.bfloat16)
        val_block = source[1].reshape(tok_rows, kv_local, HD)
        return running + jnp.einsum(
            "gqtk,kgd->gqtd", soft_bf, val_block, preferred_element_type=jnp.float32
        )

    attn_out = add_output(jnp.zeros((kv_local, q_group, tok_rows, HD), jnp.float32), sources[0], 0)
    for offset in range(1, reach + 1):

        def add_live(running):
            return add_output(running, sources[offset], offset)

        attn_out = lax.cond(is_live(offset), add_live, keep_state, attn_out)
    delta = jnp.sum(head_grad.transpose(1, 2, 0, 3).astype(jnp.float32) * attn_out, axis=-1)

    def grads_for(source, offset):
        key_block = source[0].reshape(tok_rows, kv_local, HD)
        val_block = source[1].reshape(tok_rows, kv_local, HD)
        soft = soft_weights(source, offset)
        soft_bf = soft.astype(jnp.bfloat16)
        dprob = jnp.einsum(
            "tgqd,kgd->gqtk", head_grad, val_block, preferred_element_type=jnp.float32
        )
        dscore = (soft * (dprob - delta[..., None])).astype(jnp.bfloat16)
        q_part = jnp.einsum("gqtk,kgd->tgqd", dscore, key_block, preferred_element_type=jnp.float32)
        k_part = (
            jnp.einsum("gqtk,tgqd->kgd", dscore, queries, preferred_element_type=jnp.float32)
            * scaling
        )
        v_part = jnp.einsum(
            "gqtk,tgqd->kgd", soft_bf, head_grad, preferred_element_type=jnp.float32
        )
        return (q_part, k_part, v_part)

    q_acc, k_acc, v_acc = grads_for(sources[0], 0)
    for offset in range(1, reach + 1):

        def live_grads(unused):
            return grads_for(sources[offset], offset)

        def no_grads(unused):
            return (jnp.zeros_like(q_acc), jnp.zeros_like(k_acc), jnp.zeros_like(v_acc))

        q_add, k_add, v_add = lax.cond(is_live(offset), live_grads, no_grads, 0)
        q_acc = q_acc + q_add
        sent = jnp.stack([k_add, v_add]).astype(jnp.bfloat16).reshape(2, tok_rows, kv_local * HD)
        returned = shifted(sent, "ctx", -offset)
        k_acc = k_acc + returned[0].astype(jnp.float32).reshape(tok_rows, kv_local, HD)
        v_acc = v_acc + returned[1].astype(jnp.float32).reshape(tok_rows, kv_local, HD)
    q_grad = (q_acc * scaling).astype(jnp.bfloat16).reshape(tok_rows, kv_local * q_group * HD)
    k_grad = k_acc.astype(jnp.bfloat16).reshape(tok_rows, kv_local * HD)
    v_grad = v_acc.astype(jnp.bfloat16).reshape(tok_rows, kv_local * HD)
    return (q_grad, k_grad, v_grad)


GROUP = 4
STORE_PARTS = 4
PARTS = 2
MESH = pl.DeviceIdType.MESH


def place():
    me, t = lax.axis_index("ctx"), lax.axis_index("tp")
    return me, t, me // GROUP, me % GROUP


def send(src, dst, send_sem, recv_sem, device):
    return pltpu.make_async_remote_copy(
        src_ref=src, dst_ref=dst, send_sem=send_sem, recv_sem=recv_sem,
        device_id=device, device_id_type=MESH,
    )


def arrived(ref, sem):
    pltpu.make_async_copy(ref, ref, sem).wait()


def greet(devices, groups, g, t):
    barrier = pltpu.get_barrier_semaphore()

    def signal(device):
        pl.semaphore_signal(barrier, inc=1, device_id=device, device_id_type=MESH)

    for device in devices:
        signal(device)

    @pl.when(g > 0)
    def _():
        for member in range(GROUP):
            signal(((g - 1) * GROUP + member, t))

    @pl.when(g < groups - 1)
    def _():
        for member in range(GROUP):
            signal(((g + 1) * GROUP + member, t))

    inner = jnp.where((g > 0) & (g < groups - 1), GROUP, 0)
    pl.semaphore_wait(barrier, len(devices) + GROUP + inner)


def step_kernel(
    groups, rows, q, k, v, og, w, extra, q_grad, k_grad, v_grad,
    ogb, wb, acc, head_grad, q_out, kv_out, stash, attn, sums, dq, back, returned, final, owned,
    local_sem, w_send, w_recv, up_send, down_send, og_send, og_recv, q_send, q_recv,
    kv_send, kv_recv, far_send, far_recv,
    dq_send, dq_recv, back_send, back_recv, fin_send, fin_recv, home_sem,
):
    me, t, g, l = place()
    base = g * GROUP
    wide, span = q.shape[1] // GROUP, GROUP * rows
    depth = w.shape[0]
    unit = ogb.shape[2]
    x_dev, y_l, c_l = (me, 1 - t), (l + 2) % GROUP, l + 1 - 2 * (l % 2)
    core = l % 2
    far_chip = 2 - 2 * (l // 2)
    peers = [l, c_l, far_chip, far_chip + 1]
    y_dev, c_dev = (base + y_l, t), (base + c_l, t)
    above, below = (me + GROUP, t), (me - GROUP, t)
    greet([(base + peers[j], t) for j in (1, 2, 3)] + [x_dev], groups, g, t)

    def cols(ref, index, size):
        return ref.at[:, pl.ds(pl.multiple_of(index * size, size), size)]

    narrow = wide // PARTS

    def lanes_of(ch):
        return pl.ds(pl.multiple_of(ch * narrow, HD), narrow)

    def slab_piece(group, member, ch):
        return wb.at[ch, group, pl.ds(pl.multiple_of(member * depth, depth), depth)]

    def w_cols(member, ch):
        return w.at[:, pl.ds(pl.multiple_of(member * wide + ch * narrow, HD), narrow)]

    def w_sem(group, member, ch):
        return w_recv.at[(group * GROUP + member) * PARTS + ch]

    def token_rows(ref, member):
        return ref.at[pl.ds(pl.multiple_of(member * rows, rows), rows)]

    def og_unit(tt, member, u):
        return ogb.at[tt * 2 + u, pl.ds(pl.multiple_of(member * rows, rows), rows)]

    def og_own(u):
        return og.at[:, pl.ds(u * unit, unit)]

    def og_sem(tt, member, u):
        return og_recv.at[(tt * GROUP + member) * 2 + u]

    def kv_rows(which, member):
        return kv_out.at[which, pl.ds(pl.multiple_of(span + member * rows, rows), rows)]

    sends, locals_ = [], []

    def go(copy):
        copy.start()
        sends.append(copy)

    def stay(src, dst):
        copy = pltpu.make_async_copy(src, dst, local_sem.at[len(locals_)])
        copy.start()
        locals_.append(copy)

    def up_copy(src, group, member, step, j, ch):
        return send(src, slab_piece(group, member, ch), up_send.at[(step * GROUP + j) * PARTS + ch],
                    w_sem(group, member, ch), above)

    def down_copy(src, group, member, step, j, ch):
        return send(src, slab_piece(group, member, ch), down_send.at[(step * GROUP + j) * PARTS + ch],
                    w_sem(group, member, ch), below)

    def own_send(ch):
        @pl.when(g < groups - 1)
        def _():
            up_copy(w_cols(l, ch), g, l, 0, 0, ch).start()

        @pl.when(g > 0)
        def _():
            down_copy(w_cols(l, ch), g, l, 0, 0, ch).start()

    @pl.when(core == 0)
    def _():
        for ch in range(PARTS):
            own_send(ch)

    def w_to(j):
        for ch in range(PARTS):
            go(send(w_cols(peers[j], ch), slab_piece(g, l, ch), w_send.at[(j - 1) * PARTS + ch],
                    w_sem(g, l, ch), (base + peers[j], t)))

    w_to(2)
    w_to(1)
    for which, ref in ((0, k), (1, v)):
        for j in (1, 2, 3):
            go(send(cols(ref, peers[j], HD), kv_rows(which, l), kv_send.at[which * 3 + j - 1],
                    kv_recv.at[which * GROUP + l], (base + peers[j], t)))
        stay(cols(ref, l, HD), kv_rows(which, l))
    w_to(3)
    for u in (0, 1):
        go(send(og_own(u), og_unit(t, l, u), og_send.at[u], og_sem(t, l, u), x_dev))
    for ch in range(PARTS):
        stay(w_cols(l, ch), slab_piece(g, l, ch))
    for u in (0, 1):
        go(send(og_own(u), og_unit(t, l, u), og_send.at[4 + u], og_sem(t, l, u), c_dev))
        stay(og_own(u), og_unit(t, l, u))
    for u in (1, 0):
        go(send(og_own(u), og_unit(t, l, u), og_send.at[2 + u], og_sem(t, l, u), y_dev))
    for j in (1, 2, 3):
        go(send(cols(q, peers[j], wide), token_rows(q_out, l), q_send.at[j - 1],
                q_recv.at[l], (base + peers[j], t)))
    stay(cols(q, l, wide), token_rows(q_out, l))

    @pl.when(g == 0)
    def _():
        kv_out[:, 0:span] = jnp.zeros((2, span, HD), kv_out.dtype)

    sums[...] = jnp.zeros_like(sums)

    def forward(step, ch):
        if step == 0:
            for j in range(1, GROUP):
                piece = slab_piece(g, peers[j], ch)
                arrived(piece, w_sem(g, peers[j], ch))

                @pl.when(g < groups - 1)
                def _():
                    up_copy(piece, g, peers[j], 0, j, ch).start()

                @pl.when(g > 0)
                def _():
                    down_copy(piece, g, peers[j], 0, j, ch).start()
        else:
            for j in range(GROUP):
                @pl.when((g >= step) & (g < groups - 1))
                def _():
                    piece = slab_piece(g - step, peers[j], ch)
                    arrived(piece, w_sem(g - step, peers[j], ch))
                    up_copy(piece, g - step, peers[j], step, j, ch).start()

                @pl.when((g + step < groups) & (g > 0))
                def _():
                    piece = slab_piece(g + step, peers[j], ch)
                    arrived(piece, w_sem(g + step, peers[j], ch))
                    down_copy(piece, g + step, peers[j], step, j, ch).start()

    def collect(step, ch):
        @pl.when((g >= step) & (g == groups - 1))
        def _():
            for j in range(GROUP):
                arrived(slab_piece(g - step, peers[j], ch), w_sem(g - step, peers[j], ch))

        @pl.when((g + step < groups) & (g == 0))
        def _():
            for j in range(GROUP):
                arrived(slab_piece(g + step, peers[j], ch), w_sem(g + step, peers[j], ch))

    last_slab = jnp.where(2 * g < groups, groups - 1, 0)
    early_slabs = [(last_slab + 1 + n) % groups for n in range(groups - 1)]

    def project(ch, terms, finish):
        lanes = lanes_of(ch)

        @pl.loop(0, GROUP)
        def _(i):
            part = pl.ds(pl.multiple_of(i * rows, rows), rows)
            total = acc[part] if finish and len(terms) == 1 else 0.0
            for slab in terms:
                total = total + jnp.dot(
                    ogb[slab, part], wb[ch, slab], preferred_element_type=jnp.float32)
            if finish:
                head_grad[part, lanes] = total.astype(head_grad.dtype)
            else:
                acc[part] = total

    def og_pass(tt, member, u, index, device):
        return send(og_unit(tt, member, u), og_unit(tt, member, u), og_send.at[index],
                    og_sem(tt, member, u), device)

    def og_onward(tt, member, u):
        if tt is not t:
            return [og_pass(tt, member, u, (8 if member is l else 12) + u, c_dev)]
        return [og_pass(tt, member, u, 6 + u, x_dev), og_pass(tt, member, u, 10 + u, c_dev)]

    other = 1 - t
    og_arrivals = [(tt, member, u) for tt, member in ((other, l), (t, y_l), (other, y_l))
                   for u in (0, 1)]

    def og_relay(tt, member, u):
        arrived(og_unit(tt, member, u), og_sem(tt, member, u))
        for copy in og_onward(tt, member, u):
            copy.start()

    def og_last():
        for member in (c_l, (c_l + 2) % GROUP):
            for tt in (t, 1 - t):
                for u in (0, 1):
                    arrived(og_unit(tt, member, u), og_sem(tt, member, u))

    def far_copy():
        return send(kv_out.at[:, pl.ds(span, span)], kv_out.at[:, pl.ds(0, span)],
                    far_send, far_recv, above)

    window = (GROUP + 1) * rows
    heads = wide // HD
    scaling = 1.0 / math.sqrt(HD)
    column = lax.broadcasted_iota(jnp.int32, (window, rows), 0)
    row = lax.broadcasted_iota(jnp.int32, (window, rows), 1)
    causal = column <= span + row
    lane = lax.broadcasted_iota(jnp.int32, (1, rows), 1)

    def first_of(i):
        position = g * span + i * rows + lane
        start, found = jnp.int32(0), jnp.zeros((1, rows), jnp.int32)
        for j in range(extra.shape[0]):
            found = jnp.where(position >= start, start, found)
            start = start + DOC_MIN + extra[j]
        return found

    def dot(a, b, dims):
        return lax.dot_general(a, b, ((dims[:1], dims[1:]), ((), ())),
                               preferred_element_type=jnp.float32)

    def softmax_block(i):
        r0 = pl.multiple_of(i * rows, rows)
        part, keys = pl.ds(r0, rows), pl.ds(r0, window)
        kw = kv_out[0, keys]
        vw_t = kv_out[1, keys].T
        allowed = causal & (column >= first_of(i) - ((g - 1) * span + i * rows))

        for h in range(heads):
            score = jnp.where(allowed, dot(kw, q_out[part, pl.ds(h * HD, HD)], (1, 1)), NEG_FILL)
            expd = jnp.exp((score - jnp.max(score, axis=0, keepdims=True)) * scaling)
            prob = expd * (1.0 / jnp.sum(expd, axis=0, keepdims=True))
            prob_bf = prob.astype(stash.dtype)
            stash[i * heads + h] = prob_bf
            attn[i * heads + h] = dot(vw_t, prob_bf, (1, 0))

    def keys_ready():
        for which in (0, 1):
            for j in (1, 2, 3):
                arrived(kv_rows(which, peers[j]), kv_recv.at[which * GROUP + peers[j]])
        for copy in locals_:
            copy.wait()

        @pl.when(g < groups - 1)
        def _():
            far_copy().start()

    def queries_ready():
        for j in (1, 2, 3):
            arrived(token_rows(q_out, peers[j]), q_recv.at[peers[j]])

        @pl.when(g > 0)
        def _():
            arrived(kv_out.at[:, pl.ds(0, span)], far_recv)

    @pl.when(core == 0)
    def _():
        for ch in range(PARTS):
            forward(0, ch)
        keys_ready()
        og_relay(other, l, 0)
        for ch in range(PARTS):
            forward(1, ch)
        og_relay(t, y_l, 1)
        og_relay(other, l, 1)
        og_relay(t, y_l, 0)
        for ch in range(PARTS):
            forward(2, ch)
        og_relay(other, y_l, 1)

    @pl.when(core == 1)
    def _():
        keys_ready()
        og_relay(other, l, 0)

        @pl.when(g < groups - 1)
        def _():
            far_copy().wait_send()

        own_send(0)
        forward(0, 0)
        og_relay(t, y_l, 1)
        og_relay(other, l, 1)
        own_send(1)
        forward(0, 1)
        og_relay(t, y_l, 0)
        og_relay(other, y_l, 1)
        forward(1, 0)
        forward(2, 0)
        forward(1, 1)

    queries_ready()

    @pl.loop(0, GROUP)
    def _(i):
        softmax_block(i)

        @pl.when((core == 1) & (i == 1))
        def _():
            forward(2, 1)

        @pl.when(i == 2)
        def _():
            og_relay(other, y_l, 0)

    og_last()
    sums[...] = jnp.zeros_like(sums)

    def rows_of(ref, i):
        return ref.at[pl.ds(pl.multiple_of(i * rows, rows), rows)]

    def dq_target(member, ch):
        return q_grad.at[:, pl.ds(pl.multiple_of(member * wide + ch * narrow, HD), narrow)]

    def dq_rows(i, ch):
        return dq.at[pl.ds(pl.multiple_of(i * rows, rows), rows), lanes_of(ch)]

    def dq_copy(i, ch):
        return send(dq_rows(i, ch), dq_target(l, ch), dq_send.at[i * PARTS + ch],
                    dq_recv.at[l * PARTS + ch], (base + i, t))

    def dq_stay(i, ch):
        return pltpu.make_async_copy(dq_rows(i, ch), dq_target(l, ch), home_sem.at[1 + ch])

    def part_of(ref, i):
        return ref.at[:, pl.ds(pl.multiple_of(i * rows, rows), rows)]

    def back_copy(i):
        return send(part_of(back, i), returned.at[l], back_send.at[i], back_recv.at[l],
                    (base - GROUP + i, t))

    def backward(ch):
        last = ch == PARTS - 1
        count = heads // PARTS

        @pl.loop(0, GROUP)
        def _(i):
            r0 = pl.multiple_of(i * rows, rows)
            part, keys = pl.ds(r0, rows), pl.ds(r0, window)
            vw = kv_out[1, keys]
            dk = dv = 0.0
            for n in range(count):
                h = ch * count + n
                lanes = pl.ds(pl.multiple_of(h * HD, HD), HD)
                qh, gh = q_out[part, lanes], head_grad[part, lanes]
                prob_bf = stash[i * heads + h]
                delta = jnp.sum(attn[i * heads + h] * gh.T.astype(jnp.float32), axis=0, keepdims=True)
                dprob = dot(vw, gh, (1, 1))
                dscore = (prob_bf.astype(jnp.float32) * (dprob - delta)).astype(jnp.bfloat16)
                stash[i * heads + h] = dscore
                dk = dk + dot(dscore, qh, (1, 0))
                dv = dv + dot(prob_bf, gh, (1, 0))
            sums[0, keys] += dk
            sums[1, keys] += dv

            @pl.when(last & (g > 0))
            def _():
                back[0, part] = (sums[0, part] * scaling).astype(back.dtype)
                back[1, part] = sums[1, part].astype(back.dtype)
                back_copy(i).start()

        @pl.when(last)
        def _():
            final[0] = (sums[0, span:] * scaling).astype(final.dtype)
            final[1] = sums[1, span:].astype(final.dtype)
            for i in range(GROUP):
                @pl.when(i != l)
                def _():
                    fin_copy(i).start()

                @pl.when(i == l)
                def _():
                    fin_stay(i).start()

        @pl.loop(0, GROUP)
        def _(i):
            r0 = pl.multiple_of(i * rows, rows)
            part, keys = pl.ds(r0, rows), pl.ds(r0, window)
            kw_t = kv_out[0, keys].T
            for n in range(count):
                h = ch * count + n
                grad = dot(kw_t, stash[i * heads + h], (1, 0)).T * scaling
                dq[part, pl.ds(pl.multiple_of(h * HD, HD), HD)] = grad.astype(dq.dtype)

            @pl.when(i != l)
            def _():
                dq_copy(i, ch).start()

            @pl.when(i == l)
            def _():
                dq_stay(i, ch).start()

    def fin_copy(i):
        return send(part_of(final, i), owned.at[l], fin_send.at[i], fin_recv.at[l], (base + i, t))

    def fin_stay(i):
        return pltpu.make_async_copy(part_of(final, i), owned.at[l], home_sem.at[0])

    @pl.loop(0, PARTS)
    def _(ch):
        for step in range(1, groups - 1):
            collect(step, ch)
        collect(groups - 1, ch)
        project(ch, early_slabs + [last_slab], True)
        backward(ch)

    for j in (1, 2, 3):
        for ch in range(PARTS):
            arrived(dq_target(peers[j], ch), dq_recv.at[peers[j] * PARTS + ch])
        arrived(owned.at[peers[j]], fin_recv.at[peers[j]])
    fin_stay(l).wait()

    @pl.when(g < groups - 1)
    def _():
        for member in range(GROUP):
            arrived(returned.at[member], back_recv.at[member])

    for which, out in ((0, k_grad), (1, v_grad)):
        for member in range(GROUP):
            lanes = pl.ds(member * HD, HD)

            @pl.when(g < groups - 1)
            def _():
                out[:, lanes] = (owned[member, which].astype(jnp.float32)
                                 + returned[member, which].astype(jnp.float32)).astype(out.dtype)

            @pl.when(g == groups - 1)
            def _():
                out[:, lanes] = owned[member, which]

    for i in range(GROUP):
        @pl.when(i != l)
        def _():
            for ch in range(PARTS):
                dq_copy(i, ch).wait_send()
            fin_copy(i).wait_send()

        @pl.when(i == l)
        def _():
            for ch in range(PARTS):
                dq_stay(i, ch).wait()

        @pl.when(g > 0)
        def _():
            back_copy(i).wait_send()
    for arrival in og_arrivals:
        for copy in og_onward(*arrival):
            copy.wait_send()
    for copy in sends:
        copy.wait_send()

    @pl.when((g < groups - 1) & (core == 0))
    def _():
        far_copy().wait_send()

    @pl.when(g < groups - 1)
    def _():
        for step in range(groups):
            @pl.when(g >= step)
            def _():
                for j in range(GROUP):
                    for ch in range(PARTS):
                        up_copy(slab_piece(g - step, peers[j], ch), g - step, peers[j],
                                step, j, ch).wait_send()

    @pl.when(g > 0)
    def _():
        for step in range(groups):
            @pl.when(g + step < groups)
            def _():
                for j in range(GROUP):
                    for ch in range(PARTS):
                        down_copy(slab_piece(g + step, peers[j], ch), g + step, peers[j],
                                  step, j, ch).wait_send()


def store_kernel(*refs):
    count = (len(refs) - 2) // 3
    sources, targets, buffers = refs[:count], refs[count:2 * count], refs[2 * count:3 * count]
    come, leave = refs[-2:]
    copies = []
    for i in range(count):
        rows = sources[i].shape[0] // STORE_PARTS
        for j in range(STORE_PARTS):
            part, index = pl.ds(j * rows, rows), i * STORE_PARTS + j
            copies.append((
                pltpu.make_async_copy(sources[i].at[part], buffers[i].at[part], come.at[index]),
                pltpu.make_async_copy(buffers[i].at[part], targets[i].at[part], leave.at[index]),
            ))
    for inward, _ in copies:
        inward.start()
    for inward, outward in copies:
        inward.wait()
        outward.start()
    for _, outward in copies:
        outward.wait()


def grouped(q_proj, k_proj, v_proj, out_grad, o_weight, doc_extra):
    rows, width = q_proj.shape
    groups = lax.axis_size("ctx") // GROUP
    span, wide = GROUP * rows, width // GROUP
    depth, unit = o_weight.shape[0], out_grad.shape[1] // 2
    hbm = pl.BlockSpec(memory_space=pltpu.HBM)
    vmem = pl.BlockSpec(memory_space=pltpu.VMEM)
    bf16, f32, dma = jnp.bfloat16, jnp.float32, pltpu.SemaphoreType.DMA
    line = groups * GROUP
    grads = pl.pallas_call(
        functools.partial(step_kernel, groups, rows),
        out_shape=(
            jax.ShapeDtypeStruct((rows, width), bf16),
            jax.ShapeDtypeStruct((rows, GROUP * HD), bf16),
            jax.ShapeDtypeStruct((rows, GROUP * HD), bf16),
        ),
        in_specs=[hbm] * 5 + [pl.BlockSpec(memory_space=pltpu.SMEM)],
        out_specs=(vmem, vmem, vmem),
        scratch_shapes=[
            pltpu.VMEM((groups, span, unit), bf16),
            pltpu.VMEM((PARTS, groups, GROUP * depth, wide // PARTS), bf16),
            pltpu.VMEM((span, wide // PARTS), f32),
            pltpu.VMEM((span, wide), bf16),
            pltpu.VMEM((span, wide), bf16),
            pltpu.VMEM((2, 2 * span, HD), bf16),
            pltpu.VMEM((GROUP * wide // HD, (GROUP + 1) * rows, rows), bf16),
            pltpu.VMEM((GROUP * wide // HD, HD, rows), f32),
            pltpu.VMEM((2, 2 * span, HD), f32),
            pltpu.VMEM((span, wide), bf16),
            pltpu.VMEM((2, span, HD), bf16),
            pltpu.VMEM((GROUP, 2, rows, HD), bf16),
            pltpu.VMEM((2, span, HD), bf16),
            pltpu.VMEM((GROUP, 2, rows, HD), bf16),
            dma((5 + PARTS,)), dma((3 * PARTS,)), dma((line * PARTS,)), dma((line * PARTS,)), dma((line * PARTS,)),
            dma((14,)), dma((4 * GROUP,)), dma((3,)), dma((GROUP,)),
            dma((6,)), dma((2 * GROUP,)), dma, dma,
            dma((GROUP * PARTS,)), dma((GROUP * PARTS,)), dma((GROUP,)), dma((GROUP,)),
            dma((GROUP,)), dma((GROUP,)), dma((1 + PARTS,)),
        ],
        compiler_params=pltpu.CompilerParams(
            collective_id=0, has_side_effects=True, vmem_limit_bytes=56 << 20),
    )(q_proj, k_proj, v_proj, out_grad, o_weight, doc_extra)
    return pl.pallas_call(
        store_kernel,
        out_shape=tuple(jax.ShapeDtypeStruct(grad.shape, grad.dtype) for grad in grads),
        in_specs=[pl.BlockSpec(memory_space=pl.ANY)] * 3,
        out_specs=(hbm, hbm, hbm),
        scratch_shapes=[pltpu.VMEM(grad.shape, grad.dtype) for grad in grads] + [dma((3 * STORE_PARTS,))] * 2,
    )(*grads)


def fits(mesh):
    ctx, tp = mesh.shape["ctx"], mesh.shape["tp"]
    return tp == 2 and ctx == 4 * GROUP and KVH // tp == GROUP


def solution(mesh):
    placed = (P("ctx", "tp"), P("ctx", "tp"), P("ctx", "tp"), P("ctx", "tp"), P("ctx", "tp"), P())
    return jax.shard_map(
        grouped if fits(mesh) else local,
        mesh=mesh,
        in_specs=placed,
        out_specs=(P("ctx", "tp"), P("ctx", "tp"), P("ctx", "tp")),
        check_vma=False,
    )
```

```python
import functools
import math

import jax
import jax.numpy as jnp
from jax import lax
from jax.experimental import pallas as pl
from jax.experimental.pallas import tpu as pltpu
from jax.sharding import PartitionSpec as P

H = 32
KVH = 8
HD = 128
DOC_MIN = 256
DOC_MAX = 1024


NEG_FILL = -1e30


def shifted(value, axis, steps):
    count = lax.axis_size(axis)
    leading, last = (max(0, -steps), min(count, count - steps))
    return lax.ppermute(value, axis, [(source, source + steps) for source in range(leading, last)])


def keep_state(state):
    return state


def local(q_proj, k_proj, v_proj, out_grad, o_weight, doc_extra):
    tok_rows = q_proj.shape[0]
    kv_local = k_proj.shape[1] // HD
    q_group = H // KVH
    scaling = 1.0 / math.sqrt(HD)
    reach = DOC_MAX // tok_rows
    dev_index = lax.axis_index("ctx")
    gathered = lax.all_gather(out_grad, "tp", axis=1, tiled=True)
    head_sum = jnp.dot(
        gathered,
        lax.all_gather(o_weight, "ctx", axis=0, tiled=True),
        preferred_element_type=jnp.float32,
    )
    head_grad = head_sum.astype(jnp.bfloat16).reshape(tok_rows, kv_local, q_group, HD)
    queries = q_proj.reshape(tok_rows, kv_local, q_group, HD)
    order = jnp.arange(doc_extra.shape[0], dtype=jnp.int32)
    earlier = order[:, None] > order[None, :]
    doc_starts = jnp.sum(jnp.where(earlier, DOC_MIN + doc_extra[None, :], 0), axis=1)
    position = dev_index * tok_rows + jnp.arange(tok_rows, dtype=jnp.int32)
    doc_first = jnp.max(
        jnp.where(doc_starts[None, :] <= position[:, None], doc_starts[None, :], 0), axis=1
    )
    stacked = jnp.stack([k_proj, v_proj])
    sources = [stacked]
    moving = stacked
    for offset in range(1, reach + 1):
        moving = shifted(moving, "ctx", 1)
        sources.append(moving)

    def scores_for(source, offset):
        key_block = source[0].reshape(tok_rows, kv_local, HD)
        raw_scores = (
            jnp.einsum("tgqd,kgd->gqtk", queries, key_block, preferred_element_type=jnp.float32)
            * scaling
        )
        key_pos = (dev_index - offset) * tok_rows + jnp.arange(tok_rows, dtype=jnp.int32)
        allowed = (key_pos[None, :] >= doc_first[:, None]) & (key_pos[None, :] <= position[:, None])
        return (raw_scores, allowed)

    def is_live(offset):
        return (dev_index - offset >= 0) & (doc_first[0] <= (dev_index - offset + 1) * tok_rows - 1)

    raw_scores, allowed = scores_for(sources[0], 0)
    masked = jnp.where(allowed, raw_scores, NEG_FILL)
    row_peak = jnp.max(masked, axis=-1)
    row_total = jnp.sum(jnp.exp(masked - row_peak[..., None]), axis=-1)
    for offset in range(1, reach + 1):

        def merge_block(state):
            old_peak, old_total = state
            scores_new, allowed_new = scores_for(sources[offset], offset)
            masked_new = jnp.where(allowed_new, scores_new, NEG_FILL)
            new_peak = jnp.maximum(old_peak, jnp.max(masked_new, axis=-1))
            new_total = old_total * jnp.exp(old_peak - new_peak) + jnp.sum(
                jnp.exp(masked_new - new_peak[..., None]), axis=-1
            )
            return (new_peak, new_total)

        row_peak, row_total = lax.cond(
            is_live(offset), merge_block, keep_state, (row_peak, row_total)
        )
    log_total = row_peak + jnp.log(row_total)

    def soft_weights(source, offset):
        scores_here, allowed_here = scores_for(source, offset)
        return jnp.where(allowed_here, jnp.exp(scores_here - log_total[..., None]), 0.0)

    def add_output(running, source, offset):
        soft_bf = soft_weights(source, offset).astype(jnp.bfloat16)
        val_block = source[1].reshape(tok_rows, kv_local, HD)
        return running + jnp.einsum(
            "gqtk,kgd->gqtd", soft_bf, val_block, preferred_element_type=jnp.float32
        )

    attn_out = add_output(jnp.zeros((kv_local, q_group, tok_rows, HD), jnp.float32), sources[0], 0)
    for offset in range(1, reach + 1):

        def add_live(running):
            return add_output(running, sources[offset], offset)

        attn_out = lax.cond(is_live(offset), add_live, keep_state, attn_out)
    delta = jnp.sum(head_grad.transpose(1, 2, 0, 3).astype(jnp.float32) * attn_out, axis=-1)

    def grads_for(source, offset):
        key_block = source[0].reshape(tok_rows, kv_local, HD)
        val_block = source[1].reshape(tok_rows, kv_local, HD)
        soft = soft_weights(source, offset)
        soft_bf = soft.astype(jnp.bfloat16)
        dprob = jnp.einsum(
            "tgqd,kgd->gqtk", head_grad, val_block, preferred_element_type=jnp.float32
        )
        dscore = (soft * (dprob - delta[..., None])).astype(jnp.bfloat16)
        q_part = jnp.einsum("gqtk,kgd->tgqd", dscore, key_block, preferred_element_type=jnp.float32)
        k_part = (
            jnp.einsum("gqtk,tgqd->kgd", dscore, queries, preferred_element_type=jnp.float32)
            * scaling
        )
        v_part = jnp.einsum(
            "gqtk,tgqd->kgd", soft_bf, head_grad, preferred_element_type=jnp.float32
        )
        return (q_part, k_part, v_part)

    q_acc, k_acc, v_acc = grads_for(sources[0], 0)
    for offset in range(1, reach + 1):

        def live_grads(unused):
            return grads_for(sources[offset], offset)

        def no_grads(unused):
            return (jnp.zeros_like(q_acc), jnp.zeros_like(k_acc), jnp.zeros_like(v_acc))

        q_add, k_add, v_add = lax.cond(is_live(offset), live_grads, no_grads, 0)
        q_acc = q_acc + q_add
        sent = jnp.stack([k_add, v_add]).astype(jnp.bfloat16).reshape(2, tok_rows, kv_local * HD)
        returned = shifted(sent, "ctx", -offset)
        k_acc = k_acc + returned[0].astype(jnp.float32).reshape(tok_rows, kv_local, HD)
        v_acc = v_acc + returned[1].astype(jnp.float32).reshape(tok_rows, kv_local, HD)
    q_grad = (q_acc * scaling).astype(jnp.bfloat16).reshape(tok_rows, kv_local * q_group * HD)
    k_grad = k_acc.astype(jnp.bfloat16).reshape(tok_rows, kv_local * HD)
    v_grad = v_acc.astype(jnp.bfloat16).reshape(tok_rows, kv_local * HD)
    return (q_grad, k_grad, v_grad)


GROUP = 4
STORE_PARTS = 4
PARTS = 2
MESH = pl.DeviceIdType.MESH


def place():
    me, t = lax.axis_index("ctx"), lax.axis_index("tp")
    return me, t, me // GROUP, me % GROUP


def send(src, dst, send_sem, recv_sem, device):
    return pltpu.make_async_remote_copy(
        src_ref=src, dst_ref=dst, send_sem=send_sem, recv_sem=recv_sem,
        device_id=device, device_id_type=MESH,
    )


def arrived(ref, sem):
    pltpu.make_async_copy(ref, ref, sem).wait()


def greet(devices, groups, g, t):
    barrier = pltpu.get_barrier_semaphore()

    def signal(device):
        pl.semaphore_signal(barrier, inc=1, device_id=device, device_id_type=MESH)

    for device in devices:
        signal(device)

    @pl.when(g > 0)
    def _():
        for member in range(GROUP):
            signal(((g - 1) * GROUP + member, t))

    @pl.when(g < groups - 1)
    def _():
        for member in range(GROUP):
            signal(((g + 1) * GROUP + member, t))

    inner = jnp.where((g > 0) & (g < groups - 1), GROUP, 0)
    pl.semaphore_wait(barrier, len(devices) + GROUP + inner)


def step_kernel(
    groups, rows, q, k, v, og, w, extra, q_grad, k_grad, v_grad,
    ogb, wb, acc, head_grad, q_out, kv_out, stash, attn, sums, dq, back, returned, final, owned,
    local_sem, w_send, w_recv, up_send, down_send, og_send, og_recv, q_send, q_recv,
    kv_send, kv_recv, far_send, far_recv,
    dq_send, dq_recv, back_send, back_recv, fin_send, fin_recv, home_sem,
):
    me, t, g, l = place()
    base = g * GROUP
    wide, span = q.shape[1] // GROUP, GROUP * rows
    depth = w.shape[0]
    unit = ogb.shape[2]
    x_dev, y_l, c_l = (me, 1 - t), (l + 2) % GROUP, l + 1 - 2 * (l % 2)
    core = l % 2
    far_chip = 2 - 2 * (l // 2)
    peers = [l, c_l, far_chip, far_chip + 1]
    y_dev, c_dev = (base + y_l, t), (base + c_l, t)
    above, below = (me + GROUP, t), (me - GROUP, t)
    greet([(base + peers[j], t) for j in (1, 2, 3)] + [x_dev], groups, g, t)

    def cols(ref, index, size):
        return ref.at[:, pl.ds(pl.multiple_of(index * size, size), size)]

    narrow = wide // PARTS

    def lanes_of(ch):
        return pl.ds(pl.multiple_of(ch * narrow, HD), narrow)

    def slab_piece(group, member, ch):
        return wb.at[ch, group, pl.ds(pl.multiple_of(member * depth, depth), depth)]

    def w_cols(member, ch):
        return w.at[:, pl.ds(pl.multiple_of(member * wide + ch * narrow, HD), narrow)]

    def w_sem(group, member, ch):
        return w_recv.at[(group * GROUP + member) * PARTS + ch]

    def token_rows(ref, member):
        return ref.at[pl.ds(pl.multiple_of(member * rows, rows), rows)]

    def og_unit(tt, member, u):
        return ogb.at[tt * 2 + u, pl.ds(pl.multiple_of(member * rows, rows), rows)]

    def og_own(u):
        return og.at[:, pl.ds(u * unit, unit)]

    def og_sem(tt, member, u):
        return og_recv.at[(tt * GROUP + member) * 2 + u]

    def kv_rows(which, member):
        return kv_out.at[which, pl.ds(pl.multiple_of(span + member * rows, rows), rows)]

    sends, locals_ = [], []

    def go(copy):
        copy.start()
        sends.append(copy)

    def stay(src, dst):
        copy = pltpu.make_async_copy(src, dst, local_sem.at[len(locals_)])
        copy.start()
        locals_.append(copy)

    def up_copy(src, group, member, step, j, ch):
        return send(src, slab_piece(group, member, ch), up_send.at[(step * GROUP + j) * PARTS + ch],
                    w_sem(group, member, ch), above)

    def down_copy(src, group, member, step, j, ch):
        return send(src, slab_piece(group, member, ch), down_send.at[(step * GROUP + j) * PARTS + ch],
                    w_sem(group, member, ch), below)

    def own_send(ch):
        @pl.when(g < groups - 1)
        def _():
            up_copy(w_cols(l, ch), g, l, 0, 0, ch).start()

        @pl.when(g > 0)
        def _():
            down_copy(w_cols(l, ch), g, l, 0, 0, ch).start()

    @pl.when(core == 0)
    def _():
        for ch in range(PARTS):
            own_send(ch)

    def w_to(j):
        for ch in range(PARTS):
            go(send(w_cols(peers[j], ch), slab_piece(g, l, ch), w_send.at[(j - 1) * PARTS + ch],
                    w_sem(g, l, ch), (base + peers[j], t)))

    w_to(2)
    w_to(1)
    for which, ref in ((0, k), (1, v)):
        for j in (1, 2, 3):
            go(send(cols(ref, peers[j], HD), kv_rows(which, l), kv_send.at[which * 3 + j - 1],
                    kv_recv.at[which * GROUP + l], (base + peers[j], t)))
        stay(cols(ref, l, HD), kv_rows(which, l))
    w_to(3)
    for u in (0, 1):
        go(send(og_own(u), og_unit(t, l, u), og_send.at[u], og_sem(t, l, u), x_dev))
    for ch in range(PARTS):
        stay(w_cols(l, ch), slab_piece(g, l, ch))
    for u in (0, 1):
        go(send(og_own(u), og_unit(t, l, u), og_send.at[4 + u], og_sem(t, l, u), c_dev))
        stay(og_own(u), og_unit(t, l, u))
    for u in (1, 0):
        go(send(og_own(u), og_unit(t, l, u), og_send.at[2 + u], og_sem(t, l, u), y_dev))
    for j in (1, 2, 3):
        go(send(cols(q, peers[j], wide), token_rows(q_out, l), q_send.at[j - 1],
                q_recv.at[l], (base + peers[j], t)))
    stay(cols(q, l, wide), token_rows(q_out, l))

    @pl.when(g == 0)
    def _():
        kv_out[:, 0:span] = jnp.zeros((2, span, HD), kv_out.dtype)

    sums[...] = jnp.zeros_like(sums)

    def forward(step, ch):
        if step == 0:
            for j in range(1, GROUP):
                piece = slab_piece(g, peers[j], ch)
                arrived(piece, w_sem(g, peers[j], ch))

                @pl.when(g < groups - 1)
                def _():
                    up_copy(piece, g, peers[j], 0, j, ch).start()

                @pl.when(g > 0)
                def _():
                    down_copy(piece, g, peers[j], 0, j, ch).start()
        else:
            for j in range(GROUP):
                @pl.when((g >= step) & (g < groups - 1))
                def _():
                    piece = slab_piece(g - step, peers[j], ch)
                    arrived(piece, w_sem(g - step, peers[j], ch))
                    up_copy(piece, g - step, peers[j], step, j, ch).start()

                @pl.when((g + step < groups) & (g > 0))
                def _():
                    piece = slab_piece(g + step, peers[j], ch)
                    arrived(piece, w_sem(g + step, peers[j], ch))
                    down_copy(piece, g + step, peers[j], step, j, ch).start()

    def collect(step, ch):
        @pl.when((g >= step) & (g == groups - 1))
        def _():
            for j in range(GROUP):
                arrived(slab_piece(g - step, peers[j], ch), w_sem(g - step, peers[j], ch))

        @pl.when((g + step < groups) & (g == 0))
        def _():
            for j in range(GROUP):
                arrived(slab_piece(g + step, peers[j], ch), w_sem(g + step, peers[j], ch))

    last_slab = jnp.where(2 * g < groups, groups - 1, 0)
    early_slabs = [(last_slab + 1 + n) % groups for n in range(groups - 1)]

    def project(ch, terms, finish):
        lanes = lanes_of(ch)

        @pl.loop(0, GROUP)
        def _(i):
            part = pl.ds(pl.multiple_of(i * rows, rows), rows)
            total = acc[part] if finish and len(terms) == 1 else 0.0
            for slab in terms:
                total = total + jnp.dot(
                    ogb[slab, part], wb[ch, slab], preferred_element_type=jnp.float32)
            if finish:
                head_grad[part, lanes] = total.astype(head_grad.dtype)
            else:
                acc[part] = total

    def og_pass(tt, member, u, index, device):
        return send(og_unit(tt, member, u), og_unit(tt, member, u), og_send.at[index],
                    og_sem(tt, member, u), device)

    def og_onward(tt, member, u):
        if tt is not t:
            return [og_pass(tt, member, u, (8 if member is l else 12) + u, c_dev)]
        return [og_pass(tt, member, u, 6 + u, x_dev), og_pass(tt, member, u, 10 + u, c_dev)]

    other = 1 - t
    og_arrivals = [(tt, member, u) for tt, member in ((other, l), (t, y_l), (other, y_l))
                   for u in (0, 1)]

    def og_relay(tt, member, u):
        arrived(og_unit(tt, member, u), og_sem(tt, member, u))
        for copy in og_onward(tt, member, u):
            copy.start()

    def og_last():
        for member in (c_l, (c_l + 2) % GROUP):
            for tt in (t, 1 - t):
                for u in (0, 1):
                    arrived(og_unit(tt, member, u), og_sem(tt, member, u))

    def far_copy():
        return send(kv_out.at[:, pl.ds(span, span)], kv_out.at[:, pl.ds(0, span)],
                    far_send, far_recv, above)

    window = (GROUP + 1) * rows
    heads = wide // HD
    scaling = 1.0 / math.sqrt(HD)
    column = lax.broadcasted_iota(jnp.int32, (window, rows), 0)
    row = lax.broadcasted_iota(jnp.int32, (window, rows), 1)
    causal = column <= span + row
    lane = lax.broadcasted_iota(jnp.int32, (1, rows), 1)

    def first_of(i):
        position = g * span + i * rows + lane
        start, found = jnp.int32(0), jnp.zeros((1, rows), jnp.int32)
        for j in range(extra.shape[0]):
            found = jnp.where(position >= start, start, found)
            start = start + DOC_MIN + extra[j]
        return found

    def dot(a, b, dims):
        return lax.dot_general(a, b, ((dims[:1], dims[1:]), ((), ())),
                               preferred_element_type=jnp.float32)

    def softmax_block(i):
        r0 = pl.multiple_of(i * rows, rows)
        part, keys = pl.ds(r0, rows), pl.ds(r0, window)
        kw = kv_out[0, keys]
        vw_t = kv_out[1, keys].T
        allowed = causal & (column >= first_of(i) - ((g - 1) * span + i * rows))

        for h in range(heads):
            score = jnp.where(allowed, dot(kw, q_out[part, pl.ds(h * HD, HD)], (1, 1)), NEG_FILL)
            expd = jnp.exp((score - jnp.max(score, axis=0, keepdims=True)) * scaling)
            prob = expd * (1.0 / jnp.sum(expd, axis=0, keepdims=True))
            prob_bf = prob.astype(stash.dtype)
            stash[i * heads + h] = prob_bf
            attn[i * heads + h] = dot(vw_t, prob_bf, (1, 0))

    def keys_ready():
        for which in (0, 1):
            for j in (1, 2, 3):
                arrived(kv_rows(which, peers[j]), kv_recv.at[which * GROUP + peers[j]])
        for copy in locals_:
            copy.wait()

        @pl.when(g < groups - 1)
        def _():
            far_copy().start()

    def queries_ready():
        for j in (1, 2, 3):
            arrived(token_rows(q_out, peers[j]), q_recv.at[peers[j]])

        @pl.when(g > 0)
        def _():
            arrived(kv_out.at[:, pl.ds(0, span)], far_recv)

    @pl.when(core == 0)
    def _():
        for ch in range(PARTS):
            forward(0, ch)
        keys_ready()
        og_relay(other, l, 0)
        for ch in range(PARTS):
            forward(1, ch)
        og_relay(t, y_l, 1)
        og_relay(other, l, 1)
        og_relay(t, y_l, 0)
        for ch in range(PARTS):
            forward(2, ch)
        og_relay(other, y_l, 1)

    @pl.when(core == 1)
    def _():
        keys_ready()
        og_relay(other, l, 0)

        @pl.when(g < groups - 1)
        def _():
            far_copy().wait_send()

        own_send(0)
        forward(0, 0)
        og_relay(t, y_l, 1)
        og_relay(other, l, 1)
        own_send(1)
        forward(0, 1)
        og_relay(t, y_l, 0)
        og_relay(other, y_l, 1)
        forward(1, 0)
        forward(2, 0)
        forward(1, 1)

    queries_ready()

    @pl.loop(0, GROUP)
    def _(i):
        softmax_block(i)

        @pl.when((core == 1) & (i == 1))
        def _():
            forward(2, 1)

        @pl.when(i == 2)
        def _():
            og_relay(other, y_l, 0)

    og_last()
    sums[...] = jnp.zeros_like(sums)

    def rows_of(ref, i):
        return ref.at[pl.ds(pl.multiple_of(i * rows, rows), rows)]

    def dq_target(member, ch):
        return q_grad.at[:, pl.ds(pl.multiple_of(member * wide + ch * narrow, HD), narrow)]

    def dq_rows(i, ch):
        return dq.at[pl.ds(pl.multiple_of(i * rows, rows), rows), lanes_of(ch)]

    def dq_copy(i, ch):
        return send(dq_rows(i, ch), dq_target(l, ch), dq_send.at[i * PARTS + ch],
                    dq_recv.at[l * PARTS + ch], (base + i, t))

    def dq_stay(i, ch):
        return pltpu.make_async_copy(dq_rows(i, ch), dq_target(l, ch), home_sem.at[1 + ch])

    def part_of(ref, i):
        return ref.at[:, pl.ds(pl.multiple_of(i * rows, rows), rows)]

    def back_copy(i):
        return send(part_of(back, i), returned.at[l], back_send.at[i], back_recv.at[l],
                    (base - GROUP + i, t))

    def backward(ch):
        last = ch == PARTS - 1
        count = heads // PARTS

        @pl.loop(0, GROUP)
        def _(i):
            r0 = pl.multiple_of(i * rows, rows)
            part, keys = pl.ds(r0, rows), pl.ds(r0, window)
            vw = kv_out[1, keys]
            dscores, probs = [], []
            for n in range(count):
                h = ch * count + n
                gh = head_grad[part, pl.ds(pl.multiple_of(h * HD, HD), HD)]
                prob_bf = stash[i * heads + h]
                delta = jnp.sum(attn[i * heads + h] * gh.T.astype(jnp.float32), axis=0, keepdims=True)
                dprob = dot(vw, gh, (1, 1))
                dscore = (prob_bf.astype(jnp.float32) * (dprob - delta)).astype(jnp.bfloat16)
                stash[i * heads + h] = dscore
                dscores.append(dscore)
                probs.append(prob_bf)
            q_two, g_two = (
                jnp.concatenate([ref[part, pl.ds(pl.multiple_of((ch * count + n) * HD, HD), HD)]
                                 for n in range(count)], axis=0) for ref in (q_out, head_grad))
            dk = dot(jnp.concatenate(dscores, axis=1), q_two, (1, 0))
            dv = dot(jnp.concatenate(probs, axis=1), g_two, (1, 0))
            sums[0, keys] += dk
            sums[1, keys] += dv

            @pl.when(last & (g > 0))
            def _():
                back[0, part] = (sums[0, part] * scaling).astype(back.dtype)
                back[1, part] = sums[1, part].astype(back.dtype)
                back_copy(i).start()

        @pl.when(last)
        def _():
            final[0] = (sums[0, span:] * scaling).astype(final.dtype)
            final[1] = sums[1, span:].astype(final.dtype)
            for i in range(GROUP):
                @pl.when(i != l)
                def _():
                    fin_copy(i).start()

                @pl.when(i == l)
                def _():
                    fin_stay(i).start()

        @pl.loop(0, GROUP)
        def _(i):
            r0 = pl.multiple_of(i * rows, rows)
            part, keys = pl.ds(r0, rows), pl.ds(r0, window)
            kw_t = kv_out[0, keys].T
            for n in range(count):
                h = ch * count + n
                grad = dot(kw_t, stash[i * heads + h], (1, 0)).T * scaling
                dq[part, pl.ds(pl.multiple_of(h * HD, HD), HD)] = grad.astype(dq.dtype)

            @pl.when(i != l)
            def _():
                dq_copy(i, ch).start()

            @pl.when(i == l)
            def _():
                dq_stay(i, ch).start()

    def fin_copy(i):
        return send(part_of(final, i), owned.at[l], fin_send.at[i], fin_recv.at[l], (base + i, t))

    def fin_stay(i):
        return pltpu.make_async_copy(part_of(final, i), owned.at[l], home_sem.at[0])

    @pl.loop(0, PARTS)
    def _(ch):
        for step in range(1, groups - 1):
            collect(step, ch)
        collect(groups - 1, ch)
        project(ch, early_slabs + [last_slab], True)
        backward(ch)

    for j in (1, 2, 3):
        for ch in range(PARTS):
            arrived(dq_target(peers[j], ch), dq_recv.at[peers[j] * PARTS + ch])
        arrived(owned.at[peers[j]], fin_recv.at[peers[j]])
    fin_stay(l).wait()

    @pl.when(g < groups - 1)
    def _():
        for member in range(GROUP):
            arrived(returned.at[member], back_recv.at[member])

    for which, out in ((0, k_grad), (1, v_grad)):
        for member in range(GROUP):
            lanes = pl.ds(member * HD, HD)

            @pl.when(g < groups - 1)
            def _():
                out[:, lanes] = (owned[member, which].astype(jnp.float32)
                                 + returned[member, which].astype(jnp.float32)).astype(out.dtype)

            @pl.when(g == groups - 1)
            def _():
                out[:, lanes] = owned[member, which]

    for i in range(GROUP):
        @pl.when(i != l)
        def _():
            for ch in range(PARTS):
                dq_copy(i, ch).wait_send()
            fin_copy(i).wait_send()

        @pl.when(i == l)
        def _():
            for ch in range(PARTS):
                dq_stay(i, ch).wait()

        @pl.when(g > 0)
        def _():
            back_copy(i).wait_send()
    for arrival in og_arrivals:
        for copy in og_onward(*arrival):
            copy.wait_send()
    for copy in sends:
        copy.wait_send()

    @pl.when((g < groups - 1) & (core == 0))
    def _():
        far_copy().wait_send()

    @pl.when(g < groups - 1)
    def _():
        for step in range(groups):
            @pl.when(g >= step)
            def _():
                for j in range(GROUP):
                    for ch in range(PARTS):
                        up_copy(slab_piece(g - step, peers[j], ch), g - step, peers[j],
                                step, j, ch).wait_send()

    @pl.when(g > 0)
    def _():
        for step in range(groups):
            @pl.when(g + step < groups)
            def _():
                for j in range(GROUP):
                    for ch in range(PARTS):
                        down_copy(slab_piece(g + step, peers[j], ch), g + step, peers[j],
                                  step, j, ch).wait_send()


def store_kernel(*refs):
    count = (len(refs) - 2) // 3
    sources, targets, buffers = refs[:count], refs[count:2 * count], refs[2 * count:3 * count]
    come, leave = refs[-2:]
    copies = []
    for i in range(count):
        rows = sources[i].shape[0] // STORE_PARTS
        for j in range(STORE_PARTS):
            part, index = pl.ds(j * rows, rows), i * STORE_PARTS + j
            copies.append((
                pltpu.make_async_copy(sources[i].at[part], buffers[i].at[part], come.at[index]),
                pltpu.make_async_copy(buffers[i].at[part], targets[i].at[part], leave.at[index]),
            ))
    for inward, _ in copies:
        inward.start()
    for inward, outward in copies:
        inward.wait()
        outward.start()
    for _, outward in copies:
        outward.wait()


def grouped(q_proj, k_proj, v_proj, out_grad, o_weight, doc_extra):
    rows, width = q_proj.shape
    groups = lax.axis_size("ctx") // GROUP
    span, wide = GROUP * rows, width // GROUP
    depth, unit = o_weight.shape[0], out_grad.shape[1] // 2
    hbm = pl.BlockSpec(memory_space=pltpu.HBM)
    vmem = pl.BlockSpec(memory_space=pltpu.VMEM)
    bf16, f32, dma = jnp.bfloat16, jnp.float32, pltpu.SemaphoreType.DMA
    line = groups * GROUP
    grads = pl.pallas_call(
        functools.partial(step_kernel, groups, rows),
        out_shape=(
            jax.ShapeDtypeStruct((rows, width), bf16),
            jax.ShapeDtypeStruct((rows, GROUP * HD), bf16),
            jax.ShapeDtypeStruct((rows, GROUP * HD), bf16),
        ),
        in_specs=[hbm] * 5 + [pl.BlockSpec(memory_space=pltpu.SMEM)],
        out_specs=(vmem, vmem, vmem),
        scratch_shapes=[
            pltpu.VMEM((groups, span, unit), bf16),
            pltpu.VMEM((PARTS, groups, GROUP * depth, wide // PARTS), bf16),
            pltpu.VMEM((span, wide // PARTS), f32),
            pltpu.VMEM((span, wide), bf16),
            pltpu.VMEM((span, wide), bf16),
            pltpu.VMEM((2, 2 * span, HD), bf16),
            pltpu.VMEM((GROUP * wide // HD, (GROUP + 1) * rows, rows), bf16),
            pltpu.VMEM((GROUP * wide // HD, HD, rows), f32),
            pltpu.VMEM((2, 2 * span, HD), f32),
            pltpu.VMEM((span, wide), bf16),
            pltpu.VMEM((2, span, HD), bf16),
            pltpu.VMEM((GROUP, 2, rows, HD), bf16),
            pltpu.VMEM((2, span, HD), bf16),
            pltpu.VMEM((GROUP, 2, rows, HD), bf16),
            dma((5 + PARTS,)), dma((3 * PARTS,)), dma((line * PARTS,)), dma((line * PARTS,)), dma((line * PARTS,)),
            dma((14,)), dma((4 * GROUP,)), dma((3,)), dma((GROUP,)),
            dma((6,)), dma((2 * GROUP,)), dma, dma,
            dma((GROUP * PARTS,)), dma((GROUP * PARTS,)), dma((GROUP,)), dma((GROUP,)),
            dma((GROUP,)), dma((GROUP,)), dma((1 + PARTS,)),
        ],
        compiler_params=pltpu.CompilerParams(
            collective_id=0, has_side_effects=True, vmem_limit_bytes=56 << 20),
    )(q_proj, k_proj, v_proj, out_grad, o_weight, doc_extra)
    return pl.pallas_call(
        store_kernel,
        out_shape=tuple(jax.ShapeDtypeStruct(grad.shape, grad.dtype) for grad in grads),
        in_specs=[pl.BlockSpec(memory_space=pl.ANY)] * 3,
        out_specs=(hbm, hbm, hbm),
        scratch_shapes=[pltpu.VMEM(grad.shape, grad.dtype) for grad in grads] + [dma((3 * STORE_PARTS,))] * 2,
    )(*grads)


def fits(mesh):
    ctx, tp = mesh.shape["ctx"], mesh.shape["tp"]
    return tp == 2 and ctx == 4 * GROUP and KVH // tp == GROUP


def solution(mesh):
    placed = (P("ctx", "tp"), P("ctx", "tp"), P("ctx", "tp"), P("ctx", "tp"), P("ctx", "tp"), P())
    return jax.shard_map(
        grouped if fits(mesh) else local,
        mesh=mesh,
        in_specs=placed,
        out_specs=(P("ctx", "tp"), P("ctx", "tp"), P("ctx", "tp")),
        check_vma=False,
    )
```
